1024 devices in a mesh: row: 16 (over z), col: 64 (over y, x, core).
Axes of the slice: x: 4, y: 8, z: 16, core: 2. Of those that a mesh axis runs over, the one named last changes fastest.
Arguments:
- student_in: bfloat16 [512, 8192], P('col', 'row'), may hold values from -260 to 260
- teacher_hidden: bfloat16 [512, 16384], P(None, 'col'), may hold values from -1600 to 1600
- proj: bfloat16 [16384, 8192], P('col', 'row'), may hold values from -0.046875 to 0.046875
- w_gate: bfloat16 [8192, 28672], P('row', 'col'), may hold values from -0.0625 to 0.0625
- w_up: bfloat16 [8192, 28672], P('row', 'col'), may hold values from -0.0625 to 0.0625
- w_down: bfloat16 [28672, 8192], P('col', 'row'), may hold values from -0.03125 to 0.03125
Outputs:
- grad_gate: bfloat16 [8192, 28672], P('row', 'col')
- grad_up: bfloat16 [8192, 28672], P('row', 'col')
- grad_down: bfloat16 [28672, 8192], P('col', 'row')
- distill_loss: float32 [], replicated
The draws below stay inside these ranges and needn't reach their ends.
All inputs are finite; a program needn't handle non-finite values.
Results may differ from the reference program's by a relative error of at most 0.0099.
Values may be sent and summed in bfloat16 or wider, within the bound.
A program may use at most 32 MiB of HBM per device.

```python
import jax
import jax.numpy as jnp

D = 8192
FF = 28672
KT = 16384
TOKENS = 512


def draw_student_in(key, part):
    first_key = jax.random.fold_in(key, 11)
    values = jnp.clip(1.5 * jax.random.normal(first_key, (TOKENS, D), jnp.float32), -9.0, 9.0)
    return jnp.clip(values, -260.0, 260.0).astype(jnp.bfloat16)


def draw_teacher_hidden(key, part):
    first_key = jax.random.fold_in(key, 21)
    values = jnp.clip(1.5 * jax.random.normal(first_key, (TOKENS, KT), jnp.float32), -9.0, 9.0)
    return jnp.clip(values, -1600.0, 1600.0).astype(jnp.bfloat16)


def steps_of(key, dims, shards, least, high):
    def one(position, parts):
        steps = jax.random.uniform(jax.random.fold_in(jax.random.fold_in(key, 6), position), (parts,), jnp.float32, least / len(shards), high / len(shards))
        return jnp.repeat(jnp.exp(steps), dims[position] // parts).reshape((-1,) + (1,) * (len(dims) - position - 1))

    factor_of = one(*shards[0])
    for cut in shards[1:]:
        factor_of = factor_of * one(*cut)
    return factor_of


def centred(own_key, extent, scale, bound, pieces=(), dtype=jnp.bfloat16):
    values = scale * jax.random.normal(own_key, extent, jnp.float32)
    if pieces:
        values = values * steps_of(own_key, extent, pieces, -0.22, 0.18)
    return jnp.clip(values, -bound, bound).astype(dtype)


def setup_inputs(seed: int = 0) -> dict:
    keys = jax.random.split(jax.random.key(seed), 7)
    student_in = draw_student_in(jax.random.fold_in(keys[6], 71), 0)
    teacher_hidden = draw_teacher_hidden(jax.random.fold_in(keys[6], 71), 0)
    proj = centred(keys[2], (KT, D), KT ** -0.5, 0.046875, ((0, 64), (1, 16)))
    w_gate = centred(keys[3], (D, FF), D ** -0.5, 0.0625, ((0, 16), (1, 64)))
    w_up = centred(keys[4], (D, FF), D ** -0.5, 0.0625, ((0, 16), (1, 64)))
    w_down = centred(keys[5], (FF, D), FF ** -0.5, 0.03125, ((0, 64), (1, 16)))
    return dict(student_in=student_in, teacher_hidden=teacher_hidden, proj=proj, w_gate=w_gate, w_up=w_up, w_down=w_down)


def reference(student_in, teacher_hidden, proj, w_gate, w_up, w_down):
    gate_val = jnp.dot(student_in, w_gate, preferred_element_type=jnp.float32)
    up_val = jnp.dot(student_in, w_up, preferred_element_type=jnp.float32)
    logistic = jax.nn.sigmoid(gate_val)
    silu_gate = gate_val * logistic
    hidden = (silu_gate * up_val).astype(jnp.bfloat16)
    student = student_in.astype(jnp.float32) + jnp.dot(hidden, w_down, preferred_element_type=jnp.float32)
    teacher = jnp.dot(teacher_hidden, proj, preferred_element_type=jnp.float32)
    log_probs = jax.nn.log_softmax(student, axis=-1)
    target = jax.nn.softmax(teacher, axis=-1)
    distill_loss = jnp.mean(-jnp.sum(target * log_probs, axis=-1))
    stud_grad = (jnp.exp(log_probs) - target).astype(jnp.bfloat16)
    grad_down = jnp.dot(hidden.T, stud_grad, preferred_element_type=jnp.float32).astype(jnp.bfloat16)
    hidden_grad = jnp.dot(stud_grad, w_down.T, preferred_element_type=jnp.float32)
    slope = logistic * (1.0 + gate_val * (1.0 - logistic))
    gate_grad = (hidden_grad * up_val * slope).astype(jnp.bfloat16)
    up_grad = (hidden_grad * silu_gate).astype(jnp.bfloat16)
    grad_gate = jnp.dot(student_in.T, gate_grad, preferred_element_type=jnp.float32).astype(jnp.bfloat16)
    grad_up = jnp.dot(student_in.T, up_grad, preferred_element_type=jnp.float32).astype(jnp.bfloat16)
    return (grad_gate, grad_up, grad_down, distill_loss)
```

```python
import functools

import jax
import jax.numpy as jnp
from jax import lax
from jax.experimental import pallas as pl
from jax.experimental.pallas import tpu as pltpu
from jax.sharding import PartitionSpec as P

BF16 = jnp.bfloat16
F32 = jnp.float32
MESH = pl.DeviceIdType.MESH
DMA = pltpu.SemaphoreType.DMA
NSUB = 4
STOP = 99


def body(nz, ny, nx, si_h, th_h, proj_h, wg_h, wu_h, wd_h,
         gg_o, gu_o, gd_o, loss_o, s):
    zr = nz // 2
    zl = nz - 1 - zr
    tokens = ny * nx * 16
    grp = tokens // nz // 8
    ff = wg_h.shape[1]
    half = si_h.shape[1] // 2
    rows = 128 if tokens % 128 == 0 else tokens
    nrow = tokens // rows

    z = lax.axis_index("row")
    c = lax.axis_index("col")
    core = lax.rem(c, 2)
    other = 1 - core
    x = lax.rem(c // 2, nx)
    y = c // (2 * nx)

    def wrap(v, n):
        return lax.rem(v + 2 * n, n)

    def col(yy, xx, cc):
        return (yy * nx + xx) * 2 + cc

    partner = (z, col(y, x, other))
    right = (wrap(z + 1, nz), c)
    left = (wrap(z - 1, nz), c)

    def ypeer(d):
        return (z, col(wrap(y + d, ny), x, core))

    def xpeer(e):
        return (z, col(y, wrap(x + e, nx), core))

    def zpeer(d):
        return (wrap(z + d, nz), c)

    sent = []

    def send(src, dst, sems, at, device):
        send_sem, recv_sem = sems
        copy = pltpu.make_async_remote_copy(
            src_ref=src, dst_ref=dst, send_sem=send_sem.at[at], recv_sem=recv_sem.at[at],
            device_id=device, device_id_type=MESH)
        copy.start()
        sent.append(copy)
        return copy

    def flat(value):
        return value.reshape((-1, value.shape[-1]))

    loads = []
    for k, (src, dst) in enumerate((
            (si_h, s["si"]), (th_h, s["th"]), (proj_h, s["proj"]),
            (wg_h, s["wg"]), (wu_h, s["wu"]), (wd_h, s["wd"]))):
        copy = pltpu.make_async_copy(src, dst, s["load"].at[k])
        copy.start()
        loads.append(copy)

    barrier = pltpu.get_barrier_semaphore()
    greet = [partner, right, left]
    greet += [ypeer(d) for d in range(1, ny)] + [xpeer(e) for e in range(1, nx)]
    if nz > 3:
        greet += [zpeer(d) for d in range(2, nz - 1)]
    for device in greet:
        pl.semaphore_signal(barrier, inc=1, device_id=device, device_id_type=MESH)

    loads[0].wait()
    own = s["si"][...].astype(F32)
    s["pair_out"][...] = jnp.where(core == 0, own[:, half:], own[:, :half])
    s["pair"][core] = jnp.where(core == 0, own[:, :half], own[:, half:])
    pl.semaphore_wait(barrier, len(greet))
    pair_copy = send(s["pair_out"], s["pair"].at[core], s["pair_sem"], 0, partner)

    loads[1].wait()
    loads[2].wait()

    def teach_half(h):
        weights = s["proj"][:, pl.ds(pl.multiple_of(h * half, 128), half)]

        def tile(m, carry):
            start = pl.multiple_of(m * rows, rows)
            part = jnp.dot(s["th"][pl.ds(start, rows), :], weights, preferred_element_type=F32)
            s["tp"][h, pl.ds(m * (ny // nrow), ny // nrow)] = part.reshape((ny // nrow, nx, 16, half))
            return carry

        lax.fori_loop(0, nrow, tile, 0)

    def pair_stage(part, inbox, sems):
        return [send(part.at[other, :, wrap(x + e, nx)], inbox.at[:, wrap(x + e, nx)], sems, e, partner)
                for e in range(nx)]

    def x_stage(part, inbox, outbox, box, sems, pair_copies):
        copies = []
        for e in list(range(1, nx)) + [0]:
            group = wrap(x + e, nx)
            pair_copies[e].wait_recv()
            total = part[core, :, group] + inbox[:, group]
            if e == 0:
                outbox[0] = total
            else:
                outbox[e] = total
                copies.append(send(outbox.at[e], box.at[e - 1], sems, e - 1, xpeer(e)))
        return copies

    def y_stage(outbox, box, sums, ybox, sems, copies):
        for copy in copies:
            copy.wait_recv()
        total = outbox[0]
        for e in range(1, nx):
            total = total + box[e - 1]
        sums[...] = total
        return [send(sums.at[wrap(y + d, ny)], ybox.at[d - 1], sems, d - 1, ypeer(d)) for d in range(1, ny)]

    def y_total(sums, ybox, copies):
        for copy in copies:
            copy.wait_recv()
        total = sums[y]
        for d in range(1, ny):
            total = total + ybox[d - 1]
        return total

    teach_half(other)
    teach_pair = pair_stage(s["tp"], s["t_in"], s["tc_sem"])
    teach_half(core)

    def gather_start(buf, sems):
        y_sems, x_sems, _ = sems
        y_copies = [send(buf.at[core, y, x], buf.at[core, y, x], y_sems, d - 1, ypeer(d)) for d in range(1, ny)]
        x_copies = [[send(buf.at[core, y, x], buf.at[core, y, x], x_sems, e - 1, xpeer(e)) for e in range(1, nx)]]
        return y_copies, x_copies

    def gather_finish(buf, sems, started):
        y_copies, x_copies = started
        _, x_sems, c_sems = sems
        order = sorted(range(1, ny), key=lambda d: min(d, ny - d))
        for d in order:
            y_copies[d - 1].wait_recv()
            block = buf.at[core, wrap(y - d, ny), x]
            x_copies.append([send(block, block, x_sems, d * (nx - 1) + e - 1, xpeer(e)) for e in range(1, nx)])
        c_copies = [send(buf.at[core, :, x], buf.at[core, :, x], c_sems, 0, partner)]
        for e in sorted(range(1, nx), key=lambda e: min(e, nx - e)):
            for copies in x_copies:
                copies[e - 1].wait_recv()
            block = buf.at[core, :, wrap(x - e, nx)]
            c_copies.append(send(block, block, c_sems, e, partner))
        for copy in c_copies:
            copy.wait_recv()

    pair_copy.wait_recv()
    s["tok"][core, y, x] = flat(s["pair"][...]).astype(BF16)
    tok_sems = (s["ty_sem"], s["tx_sem"], s["tk_sem"])
    started = gather_start(s["tok"], tok_sems)
    loads[3].wait()
    loads[4].wait()
    s["wcat"][:, 0:ff] = s["wg"][...]
    s["wcat"][:, ff:2 * ff] = s["wu"][...]
    gather_finish(s["tok"], tok_sems, started)

    teach_x = x_stage(s["tp"], s["t_in"], s["t_out"], s["t_box"], s["txs_sem"], teach_pair)

    yrow = ny // nrow

    def gate_tile(m, carry):
        at = pl.ds(m * yrow, yrow)
        part = jnp.dot(flat(s["tok"][0, at]), s["wcat"][0:half, :], preferred_element_type=F32)
        part += jnp.dot(flat(s["tok"][1, at]), s["wcat"][half:2 * half, :], preferred_element_type=F32)
        s["gp"][pl.ds(m * (rows // 8), rows // 8)] = part.reshape((rows // 8, 8, 2 * ff))
        return carry

    lax.fori_loop(0, nrow, gate_tile, 0)

    def ring_reduce(part, rbox, lbox, sems, nsub, between):
        r_sems, l_sems = sems
        size = grp // nsub

        def chunk(j, q):
            return pl.ds(wrap(j, nz) * grp + q * size, size)

        def piece(q):
            return pl.ds(q * size, size)

        r_copies, l_copies = [], []
        for q in range(nsub):
            r_copies.append(send(part.at[chunk(z + zr, q)], rbox.at[0, piece(q)], r_sems, q, right))
            l_copies.append(send(part.at[chunk(z - zl, q)], lbox.at[0, piece(q)], l_sems, q, left))
        for step in range(1, zr):
            between(step)
            for q in range(nsub):
                r_copies[q].wait_recv()
                rbox[step - 1, piece(q)] = rbox[step - 1, piece(q)] + part[chunk(z + zr - step, q)]
                r_copies[q] = send(rbox.at[step - 1, piece(q)], rbox.at[step, piece(q)],
                                   r_sems, step * nsub + q, right)
                if step < zl:
                    l_copies[q].wait_recv()
                    lbox[step - 1, piece(q)] = lbox[step - 1, piece(q)] + part[chunk(z - zl + step, q)]
                    l_copies[q] = send(lbox.at[step - 1, piece(q)], lbox.at[step, piece(q)],
                                       l_sems, step * nsub + q, left)
        for q in range(nsub):
            l_copies[q].wait_recv()
            r_copies[q].wait_recv()
        total = part[pl.ds(z * grp, grp)] + rbox[zr - 1] + lbox[zl - 1]
        return flat(total)

    def ring_gather(buf, sems, between):
        r_sems, l_sems = sems
        r_copy = send(buf.at[z], buf.at[z], r_sems, 0, right)
        l_copy = send(buf.at[z], buf.at[z], l_sems, 0, left)
        for step in range(1, zr + 1):
            r_copy.wait_recv()
            if step < zr:
                block = buf.at[wrap(z - step, nz)]
                r_copy = send(block, block, r_sems, step, right)
            if step <= zl:
                l_copy.wait_recv()
                if step < zl:
                    block = buf.at[wrap(z + step, nz)]
                    l_copy = send(block, block, l_sems, step, left)
            between(step)

    y_copies = []

    def teach_between(step):
        if step == zr - 1:
            y_copies.extend(y_stage(s["t_out"], s["t_box"], s["t_sum"], s["t_ybox"], s["tys_sem"], teach_x))

    gate_up = ring_reduce(s["gp"], s["g_rbox"], s["g_lbox"], (s["gr_sem"], s["gl_sem"]), NSUB, teach_between)
    gate_val = gate_up[:, 0:ff]
    up_val = gate_up[:, ff:2 * ff]
    logistic = 1.0 / (1.0 + jnp.exp(-gate_val))
    silu_gate = gate_val * logistic
    s["hid"][z] = (silu_gate * up_val).astype(BF16)
    s["silu"][...] = silu_gate
    s["slope"][...] = up_val * (logistic * (1.0 + gate_val * (1.0 - logistic)))

    def teach_finish(step):
        if step == 1:
            s["teach"][...] = y_total(s["t_sum"], s["t_ybox"], y_copies)

    loads[5].wait()
    ring_gather(s["hid"], (s["hr_sem"], s["hl_sem"]), teach_finish)

    zrow = nz // nrow

    def stud_half(h):
        weights = s["wd"][:, pl.ds(pl.multiple_of(h * half, 128), half)]

        def tile(m, carry):
            part = jnp.dot(flat(s["hid"][pl.ds(m * zrow, zrow)]), weights, preferred_element_type=F32)
            s["sp"][h, pl.ds(m * yrow, yrow)] = part.reshape((yrow, nx, 16, half))
            return carry

        lax.fori_loop(0, nrow, tile, 0)

    stud_half(other)
    stud_pair = pair_stage(s["sp"], s["s_in"], s["sc_sem"])
    stud_half(core)
    stud_x = x_stage(s["sp"], s["s_in"], s["s_out"], s["s_box"], s["sxs_sem"], stud_pair)
    stud_y = y_stage(s["s_out"], s["s_box"], s["s_sum"], s["s_ybox"], s["sys_sem"], stud_x)

    teacher = s["teach"][...]
    teach_max = jnp.max(teacher, axis=1, keepdims=True)
    teach_exp = jnp.exp(teacher - teach_max)
    teach_norm = jnp.sum(teach_exp, axis=1, keepdims=True)

    student = flat(s["pair"][...]) + y_total(s["s_sum"], s["s_ybox"], stud_y)
    stud_max = jnp.max(student, axis=1, keepdims=True)
    stud_norm = jnp.sum(jnp.exp(student - stud_max), axis=1, keepdims=True)
    cross = jnp.sum(teach_exp * student, axis=1, keepdims=True)

    lane = lax.broadcasted_iota(jnp.int32, (16, 128), 1)
    stats = jnp.where(lane == 0, stud_max, jnp.where(lane == 1, teach_max, jnp.where(
        lane == 2, stud_norm, jnp.where(lane == 3, teach_norm, cross))))

    def join(tiles):
        top = functools.reduce(jnp.maximum, tiles)
        total = jnp.zeros((16, 128), F32)
        for tile in tiles:
            scale_s = jnp.exp(tile[:, 0:1] - top[:, 0:1])
            scale_t = jnp.exp(tile[:, 1:2] - top[:, 1:2])
            total += tile * jnp.where(lane == 2, scale_s, scale_t)
        return jnp.where(lane < 2, top, total)

    s["st_pair"][core] = stats
    send(s["st_pair"].at[core], s["st_pair"].at[core], s["stc_sem"], 0, partner).wait_recv()
    s["st_z"][z] = join([s["st_pair"][0], s["st_pair"][1]])
    st_copies = [send(s["st_z"].at[z], s["st_z"].at[z], s["stz_sem"], d - 1, zpeer(d)) for d in range(1, nz)]
    for copy in st_copies:
        copy.wait_recv()
    stats = join([s["st_z"][k] for k in range(nz)])
    stud_max = stats[:, 0:1]
    teach_max = stats[:, 1:2]
    stud_norm = stats[:, 2:3]
    teach_norm = stats[:, 3:4]
    cross = stats[:, 4:5]

    stud_grad = jnp.exp(student - stud_max) / stud_norm - jnp.exp(teacher - teach_max) / teach_norm
    s["sg"][core, y, x] = stud_grad.astype(BF16)
    sg_sems = (s["gy_sem"], s["gx_sem"], s["gk_sem"])
    started = gather_start(s["sg"], sg_sems)
    token_loss = stud_max + jnp.log(stud_norm) - cross / teach_norm
    own_loss = jnp.sum(token_loss, axis=0, keepdims=True) * (1.0 / tokens)
    s["ly"][y] = jnp.broadcast_to(own_loss, (8, 128))
    ly_copies = [send(s["ly"].at[y], s["ly"].at[y], s["ly_sem"], d - 1, ypeer(d)) for d in range(1, ny)]
    gather_finish(s["sg"], sg_sems, started)

    def grad_tile(m, carry):
        at = pl.ds(m * yrow, yrow)
        nt = (((1,), (1,)), ((), ()))
        part = lax.dot_general(flat(s["sg"][0, at]), s["wd"][:, 0:half], nt, preferred_element_type=F32)
        part += lax.dot_general(flat(s["sg"][1, at]), s["wd"][:, half:2 * half], nt, preferred_element_type=F32)
        s["hp"][pl.ds(m * (rows // 8), rows // 8)] = part.reshape((rows // 8, 8, ff))
        return carry

    lax.fori_loop(0, nrow, grad_tile, 0)

    tn = (((0,), (0,)), ((), ()))
    lx_copies = []

    def down_between(step):
        if step == 1:
            for h in range(2):
                s["gd"][:, h * half:(h + 1) * half] = lax.dot_general(
                    flat(s["hid"][...]), flat(s["sg"][h]), tn, preferred_element_type=F32).astype(BF16)
            out = pltpu.make_async_copy(s["gd"], gd_o, s["out"].at[0])
            out.start()
            loads.append(out)
        if step == min(2, zr - 1):
            for copy in ly_copies:
                copy.wait_recv()
            s["lx"][x] = functools.reduce(lambda a, b: a + b, [s["ly"][k] for k in range(ny)])
            lx_copies.extend(send(s["lx"].at[x], s["lx"].at[x], s["lx_sem"], e - 1, xpeer(e)) for e in range(1, nx))

    hidden_grad = ring_reduce(s["hp"], s["h_rbox"], s["h_lbox"], (s["pr_sem"], s["pl_sem"]),
                              min(2, grp), down_between)
    s["gr"][z, 0] = (hidden_grad * s["slope"][...]).astype(BF16)
    s["gr"][z, 1] = (hidden_grad * s["silu"][...]).astype(BF16)

    def loss_finish(step):
        if step == 1:
            for copy in lx_copies:
                copy.wait_recv()
            loss_o[...] = functools.reduce(lambda a, b: a + b, [s["lx"][k] for k in range(nx)])

    ring_gather(s["gr"], (s["wr_sem"], s["wl_sem"]), loss_finish)

    outs = []
    for k, (buf, dst) in enumerate(((s["gg"], gg_o), (s["gu"], gu_o))):
        grads = flat(s["gr"][:, k])
        for h in range(2):
            buf[h * half:(h + 1) * half, :] = lax.dot_general(
                flat(s["tok"][h]), grads, tn, preferred_element_type=F32).astype(BF16)
            at = pl.ds(h * half, half)
            out = pltpu.make_async_copy(buf.at[at], dst.at[at], s["out"].at[1 + 2 * k + h])
            out.start()
            outs.append(out)
    for copy in sent:
        copy.wait_send()
    loads[6].wait()
    for out in outs:
        out.wait()


def scratch(nz, ny, nx, d_in, k_in, ff):
    zr = nz // 2
    zl = nz - 1 - zr
    tokens = ny * nx * 16
    half = d_in // 2
    tz = tokens // nz
    g = tz // 8
    V = pltpu.VMEM

    def sems(*n):
        return (DMA(n), DMA(n))

    vm = dict(
        si=V((8, d_in), BF16), th=V((tokens, k_in), BF16), proj=V((k_in, d_in), BF16),
        wg=V((d_in, ff), BF16), wu=V((d_in, ff), BF16), wd=V((ff, d_in), BF16),
        wcat=V((d_in, 2 * ff), BF16),
        pair_out=V((8, half), F32), pair=V((2, 8, half), F32),
        tok=V((2, ny, nx, 16, half), BF16), sg=V((2, ny, nx, 16, half), BF16),
        tp=V((2, ny, nx, 16, half), F32), sp=V((2, ny, nx, 16, half), F32),
        t_in=V((ny, nx, 16, half), F32), s_in=V((ny, nx, 16, half), F32),
        t_out=V((nx, ny, 16, half), F32), s_out=V((nx, ny, 16, half), F32),
        t_box=V((nx - 1, ny, 16, half), F32), s_box=V((nx - 1, ny, 16, half), F32),
        t_sum=V((ny, 16, half), F32), s_sum=V((ny, 16, half), F32),
        t_ybox=V((ny - 1, 16, half), F32), s_ybox=V((ny - 1, 16, half), F32),
        teach=V((16, half), F32),
        gp=V((tokens // 8, 8, 2 * ff), F32), hp=V((tokens // 8, 8, ff), F32),
        g_rbox=V((zr, g, 8, 2 * ff), F32), g_lbox=V((zl, g, 8, 2 * ff), F32),
        h_rbox=V((zr, g, 8, ff), F32), h_lbox=V((zl, g, 8, ff), F32),
        hid=V((nz, tz, ff), BF16), gr=V((nz, 2, tz, ff), BF16),
        silu=V((tz, ff), F32), slope=V((tz, ff), F32),
        st_pair=V((2, 16, 128), F32), st_z=V((nz, 16, 128), F32),
        ly=V((ny, 8, 128), F32), lx=V((nx, 8, 128), F32),
        gd=V((ff, d_in), BF16), gg=V((d_in, ff), BF16), gu=V((d_in, ff), BF16),
    )
    gs, hs = NSUB, min(2, g)
    sm = dict(
        pair_sem=sems(1), tc_sem=sems(nx), sc_sem=sems(nx),
        txs_sem=sems(nx - 1), sxs_sem=sems(nx - 1), tys_sem=sems(ny - 1), sys_sem=sems(ny - 1),
        ty_sem=sems(ny - 1), tx_sem=sems(ny * (nx - 1)), tk_sem=sems(nx),
        gy_sem=sems(ny - 1), gx_sem=sems(ny * (nx - 1)), gk_sem=sems(nx),
        gr_sem=sems(zr * gs), gl_sem=sems(zl * gs), hr_sem=sems(zr), hl_sem=sems(zl),
        pr_sem=sems(zr * hs), pl_sem=sems(zl * hs), wr_sem=sems(zr), wl_sem=sems(zl),
        stc_sem=sems(1), stz_sem=sems(nz - 1), ly_sem=sems(ny - 1), lx_sem=sems(nx - 1),
        load=DMA((6,)), out=DMA((5,)),
    )
    return {**vm, **sm}


def local(nz, ny, nx, student_in, teacher_hidden, proj, w_gate, w_up, w_down):
    d_in = student_in.shape[1]
    ff = w_gate.shape[1]
    names = scratch(nz, ny, nx, d_in, proj.shape[0], ff)
    tree = jax.tree.structure(names)
    leaves = jax.tree.leaves(names)

    def kernel(*refs):
        s = jax.tree.unflatten(tree, refs[10:])
        body(nz, ny, nx, *refs[:10], s)

    any_spec = pl.BlockSpec(memory_space=pl.ANY)
    out = pl.pallas_call(
        kernel,
        out_shape=(
            jax.ShapeDtypeStruct((d_in, ff), BF16), jax.ShapeDtypeStruct((d_in, ff), BF16),
            jax.ShapeDtypeStruct((ff, d_in), BF16), jax.ShapeDtypeStruct((8, 128), F32)),
        in_specs=[any_spec] * 6,
        out_specs=(any_spec, any_spec, any_spec, pl.BlockSpec(memory_space=pltpu.VMEM)),
        scratch_shapes=leaves,
        compiler_params=pltpu.CompilerParams(
            collective_id=0, has_side_effects=True, vmem_limit_bytes=56 * 1024 * 1024),
        name="distill_step",
    )(student_in, teacher_hidden, proj, w_gate, w_up, w_down)
    return out[0], out[1], out[2], out[3][0, 0]


def solution(mesh):
    nz = mesh.shape["row"]
    chips = mesh.shape["col"] // 2
    nx = 4 if chips == 32 else 2
    ny = chips // nx
    return jax.shard_map(
        functools.partial(local, nz, ny, nx),
        mesh=mesh,
        in_specs=(
            P("col", "row"),
            P(None, "col"),
            P("col", "row"),
            P("row", "col"),
            P("row", "col"),
            P("col", "row"),
        ),
        out_specs=(P("row", "col"), P("row", "col"), P("col", "row"), P()),
        check_vma=False,
    )
```

```python
import functools

import jax
import jax.numpy as jnp
from jax import lax
from jax.experimental import pallas as pl
from jax.experimental.pallas import tpu as pltpu
from jax.sharding import PartitionSpec as P

BF16 = jnp.bfloat16
F32 = jnp.float32
MESH = pl.DeviceIdType.MESH
DMA = pltpu.SemaphoreType.DMA
NSUB = 4
WSUB = 2


def body(nz, ny, nx, si_h, th_h, proj_h, wg_h, wu_h, wd_h,
         gg_o, gu_o, gd_o, loss_o, s):
    zr = nz // 2
    zl = nz - 1 - zr
    tokens = ny * nx * 16
    grp = tokens // nz // 8
    tg = tokens // nz // 16
    ff = wg_h.shape[0]
    ffp = s["wd"].shape[0]
    half = si_h.shape[1] // 2
    rows = 128 if tokens % 128 == 0 else tokens
    nrow = tokens // rows

    z = lax.axis_index("row")
    c = lax.axis_index("col")
    core = lax.rem(c, 2)
    other = 1 - core
    x = lax.rem(c // 2, nx)
    y = c // (2 * nx)

    def wrap(v, n):
        return lax.rem(v + 2 * n, n)

    def col(yy, xx, cc):
        return (yy * nx + xx) * 2 + cc

    partner = (z, col(y, x, other))
    right = (wrap(z + 1, nz), c)
    left = (wrap(z - 1, nz), c)

    def ypeer(d):
        return (z, col(wrap(y + d, ny), x, core))

    def xpeer(e):
        return (z, col(y, wrap(x + e, nx), core))

    def zpeer(d):
        return (wrap(z + d, nz), c)

    sent = []

    def send(src, dst, sems, at, device):
        send_sem, recv_sem = sems
        copy = pltpu.make_async_remote_copy(
            src_ref=src, dst_ref=dst, send_sem=send_sem.at[at], recv_sem=recv_sem.at[at],
            device_id=device, device_id_type=MESH)
        copy.start()
        sent.append(copy)
        return copy

    def flat(value):
        return value.reshape((-1, value.shape[-1]))

    loads = []
    for k, (src, dst) in enumerate((
            (si_h, s["si"]), (th_h, s["th"]), (proj_h, s["proj"]),
            (wg_h, s["wcat"].at[0:ff]), (wu_h, s["wcat"].at[ff:2 * ff]), (wd_h, s["wd"].at[0:ff]))):
        copy = pltpu.make_async_copy(src, dst, s["load"].at[k])
        copy.start()
        loads.append(copy)

    barrier = pltpu.get_barrier_semaphore()
    greet = [partner, right, left]
    greet += [ypeer(d) for d in range(1, ny)] + [xpeer(e) for e in range(1, nx)]
    greet += [zpeer(d) for d in sorted({2, nz - 2} - {1})]
    for device in greet:
        pl.semaphore_signal(barrier, inc=1, device_id=device, device_id_type=MESH)

    if ffp > ff:
        s["wd"][ff:ffp, :] = jnp.zeros((ffp - ff, 2 * half), BF16)
        s["hid"][z, :, ff:ffp] = jnp.zeros((s["hid"].shape[1], ffp - ff), BF16)

    loads[0].wait()
    own = s["si"][...].astype(F32)
    s["pair_out"][...] = jnp.where(core == 0, own[:, half:], own[:, :half])
    s["pair"][core] = jnp.where(core == 0, own[:, :half], own[:, half:])
    pl.semaphore_wait(barrier, len(greet))
    pair_copy = send(s["pair_out"], s["pair"].at[core], s["pair_sem"], 0, partner)

    loads[1].wait()
    loads[2].wait()

    def teach_half(h):
        weights = s["proj"][:, pl.ds(pl.multiple_of(h * half, 128), half)]

        def tile(m, carry):
            start = pl.multiple_of(m * rows, rows)
            part = jnp.dot(s["th"][pl.ds(start, rows), :], weights, preferred_element_type=F32)
            s["tp"][h, pl.ds(m * (ny // nrow), ny // nrow)] = part.reshape((ny // nrow, nx, 16, half))
            return carry

        lax.fori_loop(0, nrow, tile, 0)

    def pair_stage(part, inbox, sems):
        return [send(part.at[other, :, wrap(x + e, nx)], inbox.at[:, wrap(x + e, nx)], sems, e, partner)
                for e in range(nx)]

    def x_stage(part, inbox, outbox, box, sems, pair_copies):
        copies = []
        for e in list(range(1, nx)) + [0]:
            group = wrap(x + e, nx)
            pair_copies[e].wait_recv()
            total = part[core, :, group] + inbox[:, group]
            if e == 0:
                outbox[0] = total
            else:
                outbox[e] = total
                copies.append(send(outbox.at[e], box.at[e - 1], sems, e - 1, xpeer(e)))
        return copies

    def y_stage(outbox, box, sums, ybox, sems, copies):
        for copy in copies:
            copy.wait_recv()
        total = outbox[0]
        for e in range(1, nx):
            total = total + box[e - 1]
        sums[...] = total
        return [send(sums.at[wrap(y + d, ny)], ybox.at[d - 1], sems, d - 1, ypeer(d)) for d in range(1, ny)]

    def y_total(sums, ybox, copies):
        for copy in copies:
            copy.wait_recv()
        total = sums[y]
        for d in range(1, ny):
            total = total + ybox[d - 1]
        return total

    teach_half(other)
    teach_pair = pair_stage(s["tp"], s["t_in"], s["tc_sem"])
    teach_half(core)

    def gather_start(buf, sems):
        y_sems, x_sems, _ = sems
        y_copies = [send(buf.at[core, y, x], buf.at[core, y, x], y_sems, d - 1, ypeer(d)) for d in range(1, ny)]
        x_copies = [[send(buf.at[core, y, x], buf.at[core, y, x], x_sems, e - 1, xpeer(e)) for e in range(1, nx)]]
        return y_copies, x_copies

    def gather_finish(buf, sems, started):
        y_copies, x_copies = started
        _, x_sems, c_sems = sems
        order = sorted(range(1, ny), key=lambda d: min(d, ny - d))
        for d in order:
            y_copies[d - 1].wait_recv()
            block = buf.at[core, wrap(y - d, ny), x]
            x_copies.append([send(block, block, x_sems, d * (nx - 1) + e - 1, xpeer(e)) for e in range(1, nx)])
        c_copies = [send(buf.at[core, :, x], buf.at[core, :, x], c_sems, 0, partner)]
        for e in sorted(range(1, nx), key=lambda e: min(e, nx - e)):
            for copies in x_copies:
                copies[e - 1].wait_recv()
            block = buf.at[core, :, wrap(x - e, nx)]
            c_copies.append(send(block, block, c_sems, e, partner))
        for copy in c_copies:
            copy.wait_recv()

    pair_copy.wait_recv()
    s["tok"][core, y, x] = flat(s["pair"][...]).astype(BF16)
    tok_sems = (s["ty_sem"], s["tx_sem"], s["tk_sem"])
    started = gather_start(s["tok"], tok_sems)
    gather_finish(s["tok"], tok_sems, started)

    teach_x = x_stage(s["tp"], s["t_in"], s["t_out"], s["t_box"], s["txs_sem"], teach_pair)

    loads[3].wait()
    loads[4].wait()
    yrow = ny // nrow
    nt = (((1,), (1,)), ((), ()))

    def gate_tile(m, carry):
        at = pl.ds(m * yrow, yrow)
        part = lax.dot_general(flat(s["tok"][0, at]), s["wcat"][:, 0:half], nt, preferred_element_type=F32)
        part += lax.dot_general(flat(s["tok"][1, at]), s["wcat"][:, half:2 * half], nt, preferred_element_type=F32)
        s["gp"][pl.ds(m * (rows // 8), rows // 8)] = part.reshape((rows // 8, 8, 2 * ff))
        return carry

    lax.fori_loop(0, nrow, gate_tile, 0)

    def ring_reduce(part, rbox, lbox, sems, nsub, between):
        r_sems, l_sems = sems
        size = grp // nsub

        def chunk(j, q):
            return pl.ds(wrap(j, nz) * grp + q * size, size)

        def piece(q):
            return pl.ds(q * size, size)

        r_copies, l_copies = [], []
        for q in range(nsub):
            r_copies.append(send(part.at[chunk(z + zr, q)], rbox.at[0, piece(q)], r_sems, q, right))
            l_copies.append(send(part.at[chunk(z - zl, q)], lbox.at[0, piece(q)], l_sems, q, left))
        for step in range(1, zr):
            between(step)
            for q in range(nsub):
                r_copies[q].wait_recv()
                rbox[step - 1, piece(q)] = rbox[step - 1, piece(q)] + part[chunk(z + zr - step, q)]
                r_copies[q] = send(rbox.at[step - 1, piece(q)], rbox.at[step, piece(q)],
                                   r_sems, step * nsub + q, right)
                if step < zl:
                    l_copies[q].wait_recv()
                    lbox[step - 1, piece(q)] = lbox[step - 1, piece(q)] + part[chunk(z - zl + step, q)]
                    l_copies[q] = send(lbox.at[step - 1, piece(q)], lbox.at[step, piece(q)],
                                       l_sems, step * nsub + q, left)
        for q in range(nsub):
            l_copies[q].wait_recv()
            r_copies[q].wait_recv()
        total = part[pl.ds(z * grp, grp)] + rbox[zr - 1] + lbox[zl - 1]
        return flat(total)

    def ring_gather(buf, sems, nsub, between):
        r_sems, l_sems = sems
        size = buf.shape[1] // nsub

        def part(k, q):
            return buf.at[k, pl.ds(q * size, size)]

        r_copies, l_copies = [], []
        for q in range(nsub):
            r_copies.append(send(part(z, q), part(z, q), r_sems, q, right))
            l_copies.append(send(part(z, q), part(z, q), l_sems, q, left))
        for step in range(1, zr + 1):
            for q in range(nsub):
                r_copies[q].wait_recv()
                if step < zr:
                    block = part(wrap(z - step, nz), q)
                    r_copies[q] = send(block, block, r_sems, step * nsub + q, right)
                if step <= zl:
                    l_copies[q].wait_recv()
                    if step < zl:
                        block = part(wrap(z + step, nz), q)
                        l_copies[q] = send(block, block, l_sems, step * nsub + q, left)
            between(step)

    def skip_gather(buf, sems, between):
        copies = [{}, {}]
        sides = ((0, 1, zr), (1, -1, zl))

        def spread(side, sign, reach, distance):
            block = buf.at[wrap(z - sign * distance, nz)]
            for hop in (2, 1):
                if distance + hop <= reach:
                    copies[side][distance + hop] = send(
                        block, block, sems[side], distance + hop - 1, zpeer(sign * hop))

        for side in sides:
            spread(*side, 0)
        for distance in range(2, zr + 1, 2):
            for side, sign, reach in sides:
                if distance <= reach:
                    copies[side][distance].wait_recv()
                    spread(side, sign, reach, distance)
            between(distance // 2)
        for side, sign, reach in sides:
            for distance in range(1, reach + 1, 2):
                copies[side][distance].wait_recv()

    def skip_reduce(part, stage, boxes, sems, between):
        copies = [{}, {}]
        sides = ((0, 1, zr), (1, -1, zl))

        def own(j):
            return part[pl.ds(wrap(j, nz) * tg, tg)]

        def arrived(side, reach, distance):
            total = 0.0
            for hop in (1, 2):
                if distance + hop <= reach:
                    copies[side][distance + hop].wait_recv()
                    total = total + boxes[side][distance + hop - 1].astype(F32)
            return total

        def launch(side, sign, distance, value):
            hop = 2 - distance % 2
            stage[side, distance - 1] = value.astype(BF16)
            copies[side][distance] = send(
                stage.at[side, distance - 1], boxes[side].at[distance - 1], sems[side], distance - 1, zpeer(sign * hop))

        for side, sign, reach in sides:
            if reach % 2 == 0:
                launch(side, sign, reach, own(z + sign * reach))
        for distance in range(zr - 1 + zr % 2, 0, -2):
            for side, sign, reach in sides:
                if distance <= reach:
                    launch(side, sign, distance, own(z + sign * distance))
        step = 0
        for distance in range(zr, 1, -2):
            step += 1
            for side, sign, reach in sides:
                if distance < reach:
                    launch(side, sign, distance, own(z + sign * distance) + arrived(side, reach, distance))
            between(step)
        total = own(z)
        for side, sign, reach in sides:
            total = total + arrived(side, reach, 0)
        return flat(total)

    y_copies = []

    def teach_between(step):
        if step == zr - 1:
            y_copies.extend(y_stage(s["t_out"], s["t_box"], s["t_sum"], s["t_ybox"], s["tys_sem"], teach_x))

    gate_up = ring_reduce(s["gp"], s["g_rbox"], s["g_lbox"], (s["gr_sem"], s["gl_sem"]), NSUB, teach_between)
    gate_val = gate_up[:, 0:ff]
    up_val = gate_up[:, ff:2 * ff]
    logistic = 1.0 / (1.0 + jnp.exp(-gate_val))
    silu_gate = gate_val * logistic
    s["hid"][z, :, 0:ff] = (silu_gate * up_val).astype(BF16)
    s["silu"][...] = silu_gate
    s["slope"][...] = up_val * (logistic * (1.0 + gate_val * (1.0 - logistic)))

    def teach_finish(step):
        if step == 1:
            s["teach"][...] = y_total(s["t_sum"], s["t_ybox"], y_copies)

    loads[5].wait()
    skip_gather(s["hid"], (s["hr_sem"], s["hl_sem"]), teach_finish)

    zrow = nz // nrow

    def stud_half(h):
        weights = s["wd"][:, pl.ds(pl.multiple_of(h * half, 128), half)]

        def tile(m, carry):
            part = jnp.dot(flat(s["hid"][pl.ds(m * zrow, zrow)]), weights, preferred_element_type=F32)
            s["sp"][h, pl.ds(m * yrow, yrow)] = part.reshape((yrow, nx, 16, half))
            return carry

        lax.fori_loop(0, nrow, tile, 0)

    stud_half(other)
    stud_pair = pair_stage(s["sp"], s["s_in"], s["sc_sem"])
    stud_half(core)
    stud_x = x_stage(s["sp"], s["s_in"], s["s_out"], s["s_box"], s["sxs_sem"], stud_pair)
    stud_y = y_stage(s["s_out"], s["s_box"], s["s_sum"], s["s_ybox"], s["sys_sem"], stud_x)

    teacher = s["teach"][...]
    teach_max = jnp.max(teacher, axis=1, keepdims=True)
    teach_exp = jnp.exp(teacher - teach_max)
    teach_norm = jnp.sum(teach_exp, axis=1, keepdims=True)

    student = flat(s["pair"][...]) + y_total(s["s_sum"], s["s_ybox"], stud_y)
    stud_max = jnp.max(student, axis=1, keepdims=True)
    stud_norm = jnp.sum(jnp.exp(student - stud_max), axis=1, keepdims=True)
    cross = jnp.sum(teach_exp * student, axis=1, keepdims=True)

    lane = lax.broadcasted_iota(jnp.int32, (16, 128), 1)
    stats = jnp.where(lane == 0, stud_max, jnp.where(lane == 1, teach_max, jnp.where(
        lane == 2, stud_norm, jnp.where(lane == 3, teach_norm, cross))))
    stats = jnp.concatenate([stats, jnp.zeros((112, 128), F32)], axis=0).T[0:8]
    row = lax.broadcasted_iota(jnp.int32, (8, 128), 0)

    def join(tiles):
        top = functools.reduce(jnp.maximum, tiles)
        total = jnp.zeros((8, 128), F32)
        for tile in tiles:
            scale = jnp.exp(tile - top)
            total += tile * jnp.where(row == 2, scale[0:1], scale[1:2])
        return jnp.where(row < 2, top, total)

    s["st_pair"][core] = stats
    send(s["st_pair"].at[core], s["st_pair"].at[core], s["stc_sem"], 0, partner).wait_recv()
    s["st_z"][z] = join([s["st_pair"][0], s["st_pair"][1]])
    st_copies = [send(s["st_z"].at[z], s["st_z"].at[z], s["stz_sem"], d - 1, zpeer(d)) for d in range(1, nz)]
    for copy in st_copies:
        copy.wait_recv()
    stats = join([s["st_z"][k] for k in range(nz)])
    stats = jnp.concatenate([stats, jnp.zeros((120, 128), F32)], axis=0).T[0:16]
    stud_max = stats[:, 0:1]
    teach_max = stats[:, 1:2]
    stud_norm = stats[:, 2:3]
    teach_norm = stats[:, 3:4]
    cross = stats[:, 4:5]

    stud_grad = jnp.exp(student - stud_max) / stud_norm - jnp.exp(teacher - teach_max) / teach_norm
    s["sg"][core, y, x] = stud_grad.astype(BF16)
    sg_sems = (s["gy_sem"], s["gx_sem"], s["gk_sem"])
    started = gather_start(s["sg"], sg_sems)
    token_loss = stud_max + jnp.log(stud_norm) - cross / teach_norm
    own_loss = jnp.sum(token_loss, axis=0, keepdims=True) * (1.0 / tokens)
    s["ly"][y] = jnp.broadcast_to(own_loss, (8, 128))
    ly_copies = [send(s["ly"].at[y], s["ly"].at[y], s["ly_sem"], d - 1, ypeer(d)) for d in range(1, ny)]
    gather_finish(s["sg"], sg_sems, started)

    def grad_tile(m, carry):
        at = pl.ds(m * yrow, yrow)
        part = lax.dot_general(flat(s["sg"][0, at]), s["wd"][:, 0:half], nt, preferred_element_type=F32)
        part += lax.dot_general(flat(s["sg"][1, at]), s["wd"][:, half:2 * half], nt, preferred_element_type=F32)
        s["hp"][pl.ds(m * (rows // 16), rows // 16)] = part.reshape((rows // 16, 16, ffp))
        return carry

    lax.fori_loop(0, nrow, grad_tile, 0)

    tn = (((0,), (0,)), ((), ()))
    lx_copies = []

    def down_between(step):
        if step == 1:
            for h in range(2):
                s["gd"][:, h * half:(h + 1) * half] = lax.dot_general(
                    flat(s["hid"][...]), flat(s["sg"][h]), tn, preferred_element_type=F32).astype(BF16)[0:ff]
            out = pltpu.make_async_copy(s["gd"], gd_o, s["out"].at[0])
            out.start()
            loads.append(out)
        if step == max(1, zr // 2 - 1):
            for copy in ly_copies:
                copy.wait_recv()
            s["lx"][x] = functools.reduce(lambda a, b: a + b, [s["ly"][k] for k in range(ny)])
            lx_copies.extend(send(s["lx"].at[x], s["lx"].at[x], s["lx_sem"], e - 1, xpeer(e)) for e in range(1, nx))

    hidden_grad = skip_reduce(s["hp"], s["h_stage"], (s["h_rbox"], s["h_lbox"]),
                              (s["pr_sem"], s["pl_sem"]), down_between)[:, 0:ff]
    s["gr"][z, :, 0:ff] = (hidden_grad * s["slope"][...]).astype(BF16)
    s["gr"][z, :, ff:2 * ff] = (hidden_grad * s["silu"][...]).astype(BF16)

    def loss_finish(step):
        if step == 1:
            for copy in lx_copies:
                copy.wait_recv()
            loss = functools.reduce(lambda a, b: a + b, [s["lx"][k] for k in range(nx)])
            loss_o[...] = loss[0:1, 0:1]

    ring_gather(s["gr"], (s["wr_sem"], s["wl_sem"]), WSUB, loss_finish)

    outs = []
    grads = flat(s["gr"][...])
    for h in range(2):
        s["gw"][:, h * half:(h + 1) * half] = lax.dot_general(
            grads, flat(s["tok"][h]), tn, preferred_element_type=F32).astype(BF16)
    for k, dst in enumerate((gg_o, gu_o)):
        out = pltpu.make_async_copy(s["gw"].at[k * ff:(k + 1) * ff], dst, s["out"].at[1 + k])
        out.start()
        outs.append(out)
    for copy in sent:
        copy.wait_send()
    loads[6].wait()
    for out in outs:
        out.wait()


def scratch(nz, ny, nx, d_in, k_in, ff):
    zr = nz // 2
    zl = nz - 1 - zr
    tokens = ny * nx * 16
    half = d_in // 2
    tz = tokens // nz
    g = tz // 8
    tg = tz // 16
    ffp = -(-ff // 128) * 128
    V = pltpu.VMEM

    def sems(*n):
        return (DMA(n), DMA(n))

    vm = dict(
        si=V((8, d_in), BF16), th=V((tokens, k_in), BF16), proj=V((k_in, d_in), BF16),
        wcat=V((2 * ff, d_in), BF16), wd=V((ffp, d_in), BF16),
        pair_out=V((8, half), F32), pair=V((2, 8, half), F32),
        tok=V((2, ny, nx, 16, half), BF16), sg=V((2, ny, nx, 16, half), BF16),
        tp=V((2, ny, nx, 16, half), F32), sp=V((2, ny, nx, 16, half), F32),
        t_in=V((ny, nx, 16, half), F32), s_in=V((ny, nx, 16, half), F32),
        t_out=V((nx, ny, 16, half), F32), s_out=V((nx, ny, 16, half), F32),
        t_box=V((nx - 1, ny, 16, half), F32), s_box=V((nx - 1, ny, 16, half), F32),
        t_sum=V((ny, 16, half), F32), s_sum=V((ny, 16, half), F32),
        t_ybox=V((ny - 1, 16, half), F32), s_ybox=V((ny - 1, 16, half), F32),
        teach=V((16, half), F32),
        gp=V((tokens // 8, 8, 2 * ff), F32), hp=V((tokens // 16, 16, ffp), F32),
        g_rbox=V((zr, g, 8, 2 * ff), F32), g_lbox=V((zl, g, 8, 2 * ff), F32),
        h_rbox=V((zr, tg, 16, ffp), BF16), h_lbox=V((zl, tg, 16, ffp), BF16),
        h_stage=V((2, zr, tg, 16, ffp), BF16),
        hid=V((nz, tz, ffp), BF16), gr=V((nz, tz, 2 * ff), BF16),
        silu=V((tz, ff), F32), slope=V((tz, ff), F32),
        st_pair=V((2, 8, 128), F32), st_z=V((nz, 8, 128), F32),
        ly=V((ny, 8, 128), F32), lx=V((nx, 8, 128), F32),
        gd=V((ff, d_in), BF16), gw=V((2 * ff, d_in), BF16),
    )
    gs = NSUB
    sm = dict(
        pair_sem=sems(1), tc_sem=sems(nx), sc_sem=sems(nx),
        txs_sem=sems(nx - 1), sxs_sem=sems(nx - 1), tys_sem=sems(ny - 1), sys_sem=sems(ny - 1),
        ty_sem=sems(ny - 1), tx_sem=sems(ny * (nx - 1)), tk_sem=sems(nx),
        gy_sem=sems(ny - 1), gx_sem=sems(ny * (nx - 1)), gk_sem=sems(nx),
        gr_sem=sems(zr * gs), gl_sem=sems(zl * gs), hr_sem=sems(zr), hl_sem=sems(zl),
        pr_sem=sems(zr), pl_sem=sems(zl), wr_sem=sems(zr * WSUB), wl_sem=sems(zl * WSUB),
        stc_sem=sems(1), stz_sem=sems(nz - 1), ly_sem=sems(ny - 1), lx_sem=sems(nx - 1),
        load=DMA((6,)), out=DMA((3,)),
    )
    return {**vm, **sm}


def local(nz, ny, nx, student_in, teacher_hidden, proj, w_gate, w_up, w_down):
    w_gate, w_up = w_gate.T, w_up.T
    d_in = student_in.shape[1]
    ff = w_gate.shape[0]
    names = scratch(nz, ny, nx, d_in, proj.shape[0], ff)
    tree = jax.tree.structure(names)
    leaves = jax.tree.leaves(names)

    def kernel(*refs):
        s = jax.tree.unflatten(tree, refs[10:])
        body(nz, ny, nx, *refs[:10], s)

    any_spec = pl.BlockSpec(memory_space=pl.ANY)
    out = pl.pallas_call(
        kernel,
        out_shape=(
            jax.ShapeDtypeStruct((ff, d_in), BF16), jax.ShapeDtypeStruct((ff, d_in), BF16),
            jax.ShapeDtypeStruct((ff, d_in), BF16), jax.ShapeDtypeStruct((1, 1), F32)),
        in_specs=[any_spec] * 6,
        out_specs=(any_spec, any_spec, any_spec, pl.BlockSpec(memory_space=pltpu.VMEM)),
        scratch_shapes=leaves,
        compiler_params=pltpu.CompilerParams(
            collective_id=0, has_side_effects=True, vmem_limit_bytes=56 * 1024 * 1024),
        name="distill_step",
    )(student_in, teacher_hidden, proj, w_gate, w_up, w_down)
    return out[0].T, out[1].T, out[2], out[3].reshape(())


def solution(mesh):
    nz = mesh.shape["row"]
    chips = mesh.shape["col"] // 2
    nx = 4 if chips == 32 else 2
    ny = chips // nx
    return jax.shard_map(
        functools.partial(local, nz, ny, nx),
        mesh=mesh,
        in_specs=(
            P("col", "row"),
            P(None, "col"),
            P("col", "row"),
            P("row", "col"),
            P("row", "col"),
            P("col", "row"),
        ),
        out_specs=(P("row", "col"), P("row", "col"), P("col", "row"), P()),
        check_vma=False,
    )
```

```python
import functools

import jax
import jax.numpy as jnp
from jax import lax
from jax.experimental import pallas as pl
from jax.experimental.pallas import tpu as pltpu
from jax.sharding import PartitionSpec as P

BF16 = jnp.bfloat16
F32 = jnp.float32
MESH = pl.DeviceIdType.MESH
DMA = pltpu.SemaphoreType.DMA
NSUB = 4


def body(nz, ny, nx, si_h, th_h, proj_h, wg_h, wu_h, wd_h,
         gg_o, gu_o, gd_o, loss_o, s):
    zr = nz // 2
    zl = nz - 1 - zr
    tokens = ny * nx * 16
    grp = tokens // nz // 8
    tg = tokens // nz // 16
    tz = tokens // nz
    ff = wg_h.shape[0]
    ffp = s["wd"].shape[0]
    half = si_h.shape[1] // 2
    rows = 128 if tokens % 128 == 0 else tokens
    nrow = tokens // rows

    z = lax.axis_index("row")
    c = lax.axis_index("col")
    core = lax.rem(c, 2)
    other = 1 - core
    x = lax.rem(c // 2, nx)
    y = c // (2 * nx)

    def wrap(v, n):
        return lax.rem(v + 2 * n, n)

    def col(yy, xx, cc):
        return (yy * nx + xx) * 2 + cc

    partner = (z, col(y, x, other))
    right = (wrap(z + 1, nz), c)
    left = (wrap(z - 1, nz), c)

    def ypeer(d):
        return (z, col(wrap(y + d, ny), x, core))

    def xpeer(e):
        return (z, col(y, wrap(x + e, nx), core))

    def zpeer(d):
        return (wrap(z + d, nz), c)

    sent = []

    def send(src, dst, sems, at, device):
        send_sem, recv_sem = sems
        copy = pltpu.make_async_remote_copy(
            src_ref=src, dst_ref=dst, send_sem=send_sem.at[at], recv_sem=recv_sem.at[at],
            device_id=device, device_id_type=MESH)
        copy.start()
        sent.append(copy)
        return copy

    def flat(value):
        return value.reshape((-1, value.shape[-1]))

    loads = []
    for k, (src, dst) in enumerate((
            (si_h, s["si"]), (th_h, s["th"]), (proj_h, s["proj"]),
            (wg_h, s["wcat"].at[0:ff]), (wu_h, s["wcat"].at[ff:2 * ff]), (wd_h, s["wd"].at[0:ff]))):
        copy = pltpu.make_async_copy(src, dst, s["load"].at[k])
        copy.start()
        loads.append(copy)

    barrier = pltpu.get_barrier_semaphore()
    greet = [partner, right, left]
    greet += [ypeer(d) for d in range(1, ny)] + [xpeer(e) for e in range(1, nx)]
    greet += [zpeer(d) for d in sorted({2, nz - 2} - {1})]
    for device in greet:
        pl.semaphore_signal(barrier, inc=1, device_id=device, device_id_type=MESH)

    if ffp > ff:
        s["wd"][ff:ffp, :] = jnp.zeros((ffp - ff, 2 * half), BF16)
        s["hid"][z, :, ff:ffp] = jnp.zeros((s["hid"].shape[1], ffp - ff), BF16)
        s["ab"][z, :, ff:ffp] = jnp.zeros((s["ab"].shape[1], ffp - ff), BF16)

    loads[0].wait()
    own = s["si"][...].astype(F32)
    s["pair_out"][...] = jnp.where(core == 0, own[:, half:], own[:, :half])
    s["pair"][core] = jnp.where(core == 0, own[:, :half], own[:, half:])
    pl.semaphore_wait(barrier, len(greet))
    pair_copy = send(s["pair_out"], s["pair"].at[core], s["pair_sem"], 0, partner)

    loads[1].wait()
    loads[2].wait()

    def teach_half(h):
        weights = s["proj"][:, pl.ds(pl.multiple_of(h * half, 128), half)]

        def tile(m, carry):
            start = pl.multiple_of(m * rows, rows)
            part = jnp.dot(s["th"][pl.ds(start, rows), :], weights, preferred_element_type=F32)
            s["tp"][h, pl.ds(m * (ny // nrow), ny // nrow)] = part.reshape((ny // nrow, nx, 16, half))
            return carry

        lax.fori_loop(0, nrow, tile, 0)

    def pair_stage(part, inbox, sems):
        return [send(part.at[other, :, wrap(x + e, nx)], inbox.at[:, wrap(x + e, nx)], sems, e, partner)
                for e in range(nx)]

    def x_stage(part, inbox, outbox, box, sems, pair_copies):
        copies = []
        for e in list(range(1, nx)) + [0]:
            group = wrap(x + e, nx)
            pair_copies[e].wait_recv()
            total = part[core, :, group] + inbox[:, group]
            if e == 0:
                outbox[0] = total
            else:
                outbox[e] = total
                copies.append(send(outbox.at[e], box.at[e - 1], sems, e - 1, xpeer(e)))
        return copies

    def y_stage(outbox, box, sums, ybox, sems, copies):
        for copy in copies:
            copy.wait_recv()
        total = outbox[0]
        for e in range(1, nx):
            total = total + box[e - 1]
        sums[...] = total
        return [send(sums.at[wrap(y + d, ny)], ybox.at[d - 1], sems, d - 1, ypeer(d)) for d in range(1, ny)]

    def y_total(sums, ybox, copies):
        for copy in copies:
            copy.wait_recv()
        total = sums[y]
        for d in range(1, ny):
            total = total + ybox[d - 1]
        return total

    teach_half(other)
    teach_pair = pair_stage(s["tp"], s["t_in"], s["tc_sem"])
    teach_half(core)

    def gather_start(buf, sems):
        y_sems, x_sems, _ = sems
        y_copies = [send(buf.at[core, y, x], buf.at[core, y, x], y_sems, d - 1, ypeer(d)) for d in range(1, ny)]
        x_copies = [[send(buf.at[core, y, x], buf.at[core, y, x], x_sems, e - 1, xpeer(e)) for e in range(1, nx)]]
        return y_copies, x_copies

    def gather_finish(buf, sems, started):
        y_copies, x_copies = started
        _, x_sems, c_sems = sems
        order = sorted(range(1, ny), key=lambda d: min(d, ny - d))
        for d in order:
            y_copies[d - 1].wait_recv()
            block = buf.at[core, wrap(y - d, ny), x]
            x_copies.append([send(block, block, x_sems, d * (nx - 1) + e - 1, xpeer(e)) for e in range(1, nx)])
        c_copies = [send(buf.at[core, :, x], buf.at[core, :, x], c_sems, 0, partner)]
        for e in sorted(range(1, nx), key=lambda e: min(e, nx - e)):
            for copies in x_copies:
                copies[e - 1].wait_recv()
            block = buf.at[core, :, wrap(x - e, nx)]
            c_copies.append(send(block, block, c_sems, e, partner))
        for copy in c_copies:
            copy.wait_recv()

    pair_copy.wait_recv()
    s["tok"][core, y, x] = flat(s["pair"][...]).astype(BF16)
    tok_sems = (s["ty_sem"], s["tx_sem"], s["tk_sem"])
    started = gather_start(s["tok"], tok_sems)
    gather_finish(s["tok"], tok_sems, started)

    loads[3].wait()
    loads[4].wait()
    yrow = ny // nrow
    nt = (((1,), (1,)), ((), ()))

    def gate_tile(m, carry):
        at = pl.ds(m * yrow, yrow)
        part = lax.dot_general(flat(s["tok"][0, at]), s["wcat"][:, 0:half], nt, preferred_element_type=F32)
        part += lax.dot_general(flat(s["tok"][1, at]), s["wcat"][:, half:2 * half], nt, preferred_element_type=F32)
        s["gp"][pl.ds(m * (rows // 8), rows // 8)] = part.reshape((rows // 8, 8, 2 * ff))
        return carry

    lax.fori_loop(0, nrow, gate_tile, 0)

    def ring_reduce(part, rbox, lbox, sems, nsub, between):
        r_sems, l_sems = sems
        size = grp // nsub

        def chunk(j, q):
            return (pl.ds(wrap(j, nz) * grp + q // 2 * size, size), slice(None), lanes[q % 2])

        def piece(step, q):
            return (step, pl.ds(q // 2 * size, size), slice(None), lanes[q % 2])

        width = part.shape[2]
        cut = -(-width // 256) * 128
        lanes = (slice(0, cut), slice(cut, width))
        r_copies, l_copies = [], []
        for q in range(2 * nsub):
            r_copies.append(send(part.at[chunk(z + zr, q)], rbox.at[piece(0, q)], r_sems, q, right))
            l_copies.append(send(part.at[chunk(z - zl, q)], lbox.at[piece(0, q)], l_sems, q, left))
        for step in range(1, zr):
            between(step)
            for q in range(2 * nsub):
                was, now = piece(step - 1, q), piece(step, q)
                at = step * 2 * nsub + q
                r_copies[q].wait_recv()
                rbox[was] = rbox[was] + part[chunk(z + zr - step, q)]
                r_copies[q] = send(rbox.at[was], rbox.at[now], r_sems, at, right)
                if step < zl:
                    l_copies[q].wait_recv()
                    lbox[was] = lbox[was] + part[chunk(z - zl + step, q)]
                    l_copies[q] = send(lbox.at[was], lbox.at[now], l_sems, at, left)
        for q in range(2 * nsub):
            l_copies[q].wait_recv()
            r_copies[q].wait_recv()
        total = part[pl.ds(z * grp, grp)] + rbox[zr - 1] + lbox[zl - 1]
        return flat(total)

    def skip_gather(buf, sems):
        copies = [{}, {}]
        sides = ((0, 1, zr), (1, -1, zl))

        def spread(side, sign, reach, distance):
            block = buf.at[wrap(z - sign * distance, nz)]
            for hop in (2, 1):
                if distance + hop <= reach:
                    copies[side][distance + hop] = send(
                        block, block, sems[side], distance + hop - 1, zpeer(sign * hop))

        for side in sides:
            spread(*side, 0)
        yield
        for distance in range(2, zr + 1, 2):
            for side, sign, reach in sides:
                if distance <= reach:
                    copies[side][distance].wait_recv()
                    spread(side, sign, reach, distance)
            yield
        for side, sign, reach in sides:
            for distance in range(1, reach + 1, 2):
                copies[side][distance].wait_recv()

    def skip_reduce(part, stage, boxes, sems, between):
        copies = [{}, {}]
        sides = ((0, 1, zr), (1, -1, zl))

        def own(j):
            return part[pl.ds(wrap(j, nz) * tg, tg)]

        def arrived(side, reach, distance):
            total = 0.0
            for hop in (1, 2):
                if distance + hop <= reach:
                    copies[side][distance + hop].wait_recv()
                    total = total + boxes[side][distance + hop - 1].astype(F32)
            return total

        def launch(side, sign, distance, value):
            hop = 2 - distance % 2
            stage[side, distance - 1] = value.astype(BF16)
            copies[side][distance] = send(
                stage.at[side, distance - 1], boxes[side].at[distance - 1], sems[side], distance - 1, zpeer(sign * hop))

        for side, sign, reach in sides:
            if reach % 2 == 0:
                launch(side, sign, reach, own(z + sign * reach))
        for distance in range(zr - 1 + zr % 2, 0, -2):
            for side, sign, reach in sides:
                if distance <= reach:
                    launch(side, sign, distance, own(z + sign * distance))
        step = 0
        for distance in range(zr, 1, -2):
            step += 1
            for side, sign, reach in sides:
                if distance < reach:
                    launch(side, sign, distance, own(z + sign * distance) + arrived(side, reach, distance))
            between(step)
        total = own(z)
        for side, sign, reach in sides:
            total = total + arrived(side, reach, 0)
        return flat(total)

    teach_x, y_copies = [], []

    def teach_between(step):
        if step == 1:
            teach_x.extend(x_stage(s["tp"], s["t_in"], s["t_out"], s["t_box"], s["txs_sem"], teach_pair))
        if step == zr - 1:
            y_copies.extend(y_stage(s["t_out"], s["t_box"], s["t_sum"], s["t_ybox"], s["tys_sem"], teach_x))

    gate_up = ring_reduce(s["gp"], s["g_rbox"], s["g_lbox"], (s["gr_sem"], s["gl_sem"]), NSUB, teach_between)
    gate_val = gate_up[:, 0:ff]
    up_val = gate_up[:, ff:2 * ff]
    logistic = 1.0 / (1.0 + jnp.exp(-gate_val))
    silu_gate = gate_val * logistic
    s["hid"][z, :, 0:ff] = (silu_gate * up_val).astype(BF16)
    gather = skip_gather(s["hid"], (s["hr_sem"], s["hl_sem"]))
    next(gather)
    slope = up_val * (logistic * (1.0 + gate_val * (1.0 - logistic)))
    s["ab"][z, 0:tz, 0:ff] = slope.astype(BF16)
    s["ab"][z, tz:2 * tz, 0:ff] = silu_gate.astype(BF16)
    loads[5].wait()
    next(gather)
    s["teach"][...] = y_total(s["t_sum"], s["t_ybox"], y_copies)
    for _ in gather:
        pass

    zrow = nz // nrow

    def stud_half(h):
        weights = s["wd"][:, pl.ds(pl.multiple_of(h * half, 128), half)]

        def tile(m, carry):
            part = jnp.dot(flat(s["hid"][pl.ds(m * zrow, zrow)]), weights, preferred_element_type=F32)
            s["sp"][h, pl.ds(m * yrow, yrow)] = part.reshape((yrow, nx, 16, half))
            return carry

        lax.fori_loop(0, nrow, tile, 0)

    factors = skip_gather(s["ab"], (s["ar_sem"], s["al_sem"]))
    order = sorted(range(ny), key=lambda d: -min(d, ny - d))
    stud_half(other)
    pair_copies = {}
    for d in order:
        yy = wrap(y + d, ny)
        pair_copies[d] = send(s["sp"].at[other, yy], s["s_in"].at[yy], s["sc_sem"], d, partner)
    next(factors)
    stud_half(core)
    x_copies = {}
    for d in order:
        yy = wrap(y + d, ny)
        pair_copies[d].wait_recv()
        x_copies[d] = []
        for e in range(1, nx):
            xx = wrap(x + e, nx)
            s["s_out"][e, yy] = s["sp"][core, yy, xx] + s["s_in"][yy, xx]
            x_copies[d].append(send(s["s_out"].at[e, yy], s["s_box"].at[e - 1, yy], s["sxs_sem"],
                                    d * (nx - 1) + e - 1, xpeer(e)))
        s["s_out"][0, yy] = s["sp"][core, yy, x] + s["s_in"][yy, x]
    next(factors)
    stud_y = []
    for d in order:
        yy = wrap(y + d, ny)
        total = s["s_out"][0, yy]
        for e in range(1, nx):
            x_copies[d][e - 1].wait_recv()
            total = total + s["s_box"][e - 1, yy]
        s["s_sum"][yy] = total
        if d:
            stud_y.append((d, send(s["s_sum"].at[yy], s["s_ybox"].at[d - 1], s["sys_sem"], d - 1, ypeer(d))))
    stud_y = [copy for _, copy in sorted(stud_y, key=lambda pair: pair[0])]
    if zr > 2:
        next(factors)

    teacher = s["teach"][...]
    teach_max = jnp.max(teacher, axis=1, keepdims=True)
    teach_exp = jnp.exp(teacher - teach_max)
    teach_norm = jnp.sum(teach_exp, axis=1, keepdims=True)

    student = flat(s["pair"][...]) + y_total(s["s_sum"], s["s_ybox"], stud_y)
    stud_max = jnp.max(student, axis=1, keepdims=True)
    stud_norm = jnp.sum(jnp.exp(student - stud_max), axis=1, keepdims=True)
    cross = jnp.sum(teach_exp * student, axis=1, keepdims=True)

    lane = lax.broadcasted_iota(jnp.int32, (16, 128), 1)
    stats = jnp.where(lane == 0, stud_max, jnp.where(lane == 1, teach_max, jnp.where(
        lane == 2, stud_norm, jnp.where(lane == 3, teach_norm, cross))))
    stats = jnp.concatenate([stats, jnp.zeros((112, 128), F32)], axis=0).T[0:8]
    line = stats[0:1]
    for k in range(1, 5):
        line = line + pltpu.roll(stats, 16 * k, 1)[k:k + 1]
    mine = 2 * z + core
    s["st"][mine] = line
    st_copies = []
    for d in range(nz):
        for k, cc in enumerate((core, other)):
            if d or k:
                st_copies.append(send(s["st"].at[mine], s["st"].at[mine], s["st_sem"], 2 * d + k - 1,
                                      (wrap(z + d, nz), col(y, x, cc))))
    if zr > 3:
        next(factors)
    for copy in st_copies:
        copy.wait_recv()
    lines = s["st"][...].reshape((2 * nz, 128))
    top = jnp.max(lines, axis=0, keepdims=True)
    scale = jnp.exp(lines - top)
    wide = lax.broadcasted_iota(jnp.int32, (2 * nz, 128), 1)
    scale = jnp.where(wide < 64, pltpu.roll(scale, 32, 1), pltpu.roll(scale, 48, 1))
    total = jnp.sum(lines * scale, axis=0, keepdims=True)
    row = lax.broadcasted_iota(jnp.int32, (8, 128), 0)
    line = jnp.broadcast_to(jnp.where(wide[0:1] < 32, top, total), (8, 128))
    stats = line
    for k in range(1, 5):
        stats = jnp.where(row == k, pltpu.roll(line, 128 - 16 * k, 1), stats)
    stats = jnp.concatenate([stats, jnp.zeros((120, 128), F32)], axis=0).T[0:16]
    stud_max = stats[:, 0:1]
    teach_max = stats[:, 1:2]
    stud_norm = stats[:, 2:3]
    teach_norm = stats[:, 3:4]
    cross = stats[:, 4:5]

    stud_grad = jnp.exp(student - stud_max) / stud_norm - jnp.exp(teacher - teach_max) / teach_norm
    s["sg"][core, y, x] = stud_grad.astype(BF16)
    sg_sems = (s["gy_sem"], s["gx_sem"], s["gk_sem"])
    started = gather_start(s["sg"], sg_sems)
    token_loss = stud_max + jnp.log(stud_norm) - cross / teach_norm
    own_loss = jnp.sum(token_loss, axis=0, keepdims=True) * (1.0 / tokens)
    s["ly"][y] = jnp.broadcast_to(own_loss, (8, 128))
    ly_copies = [send(s["ly"].at[y], s["ly"].at[y], s["ly_sem"], d - 1, ypeer(d)) for d in range(1, ny)]
    gather_finish(s["sg"], sg_sems, started)

    def grad_tile(m, carry):
        at = pl.ds(m * yrow, yrow)
        part = lax.dot_general(flat(s["sg"][0, at]), s["wd"][:, 0:half], nt, preferred_element_type=F32)
        part += lax.dot_general(flat(s["sg"][1, at]), s["wd"][:, half:2 * half], nt, preferred_element_type=F32)
        s["hp"][pl.ds(m * (rows // 16), rows // 16)] = part.reshape((rows // 16, 16, ffp))
        return carry

    lax.fori_loop(0, nrow, grad_tile, 0)

    tn = (((0,), (0,)), ((), ()))
    lx_copies = []

    def down_between(step):
        if step <= 2:
            h = step - 1
            s["gd"][:, h * half:(h + 1) * half] = lax.dot_general(
                flat(s["hid"][...]), flat(s["sg"][h]), tn, preferred_element_type=F32).astype(BF16)[0:ff]
        if step == zr // 2:
            for copy in ly_copies:
                copy.wait_recv()
            s["lx"][x] = functools.reduce(lambda a, b: a + b, [s["ly"][k] for k in range(ny)])
            lx_copies.extend(send(s["lx"].at[x], s["lx"].at[x], s["lx_sem"], e - 1, xpeer(e)) for e in range(1, nx))

    hidden_grad = skip_reduce(s["hp"], s["h_stage"], (s["h_rbox"], s["h_lbox"]),
                              (s["pr_sem"], s["pl_sem"]), down_between)
    s["hg"][z] = hidden_grad.astype(BF16)
    gather = skip_gather(s["hg"], (s["wr_sem"], s["wl_sem"]))
    next(gather)
    for _ in factors:
        pass
    if zr < 4:
        for h in range(zr // 2, 2):
            down_between(h + 1)
    out = pltpu.make_async_copy(s["gd"], gd_o, s["out"].at[0])
    out.start()
    loads.append(out)
    next(gather)
    for copy in lx_copies:
        copy.wait_recv()
    loss = functools.reduce(lambda a, b: a + b, [s["lx"][k] for k in range(nx)])
    loss_o[...] = loss[0:1, 0:1]
    for _ in gather:
        pass

    def factor_tile(m, carry):
        at = pl.ds(m * zrow, zrow)
        grad = s["hg"][at].astype(F32)
        for k in range(2):
            factor = s["ab"][at, k * tz:(k + 1) * tz].astype(F32)
            s["gr"][k, at] = (grad * factor).astype(BF16)
        return carry

    lax.fori_loop(0, nrow, factor_tile, 0)

    outs = []
    for k, dst in enumerate((gg_o, gu_o)):
        for h in range(2):
            s["gw"][k, :, h * half:(h + 1) * half] = lax.dot_general(
                flat(s["gr"][k]), flat(s["tok"][h]), tn, preferred_element_type=F32).astype(BF16)[0:ff]
        out = pltpu.make_async_copy(s["gw"].at[k], dst, s["out"].at[1 + k])
        out.start()
        outs.append(out)
    for copy in sent:
        copy.wait_send()
    loads[6].wait()
    for out in outs:
        out.wait()


def scratch(nz, ny, nx, d_in, k_in, ff):
    zr = nz // 2
    zl = nz - 1 - zr
    tokens = ny * nx * 16
    half = d_in // 2
    tz = tokens // nz
    g = tz // 8
    tg = tz // 16
    ffp = -(-ff // 128) * 128
    V = pltpu.VMEM

    def sems(*n):
        return (DMA(n), DMA(n))

    vm = dict(
        si=V((8, d_in), BF16), th=V((tokens, k_in), BF16), proj=V((k_in, d_in), BF16),
        wcat=V((2 * ff, d_in), BF16), wd=V((ffp, d_in), BF16),
        pair_out=V((8, half), F32), pair=V((2, 8, half), F32),
        tok=V((2, ny, nx, 16, half), BF16), sg=V((2, ny, nx, 16, half), BF16),
        tp=V((2, ny, nx, 16, half), F32), sp=V((2, ny, nx, 16, half), F32),
        t_in=V((ny, nx, 16, half), F32), s_in=V((ny, nx, 16, half), F32),
        t_out=V((nx, ny, 16, half), F32), s_out=V((nx, ny, 16, half), F32),
        t_box=V((nx - 1, ny, 16, half), F32), s_box=V((nx - 1, ny, 16, half), F32),
        t_sum=V((ny, 16, half), F32), s_sum=V((ny, 16, half), F32),
        t_ybox=V((ny - 1, 16, half), F32), s_ybox=V((ny - 1, 16, half), F32),
        teach=V((16, half), F32),
        gp=V((tokens // 8, 8, 2 * ff), F32), hp=V((tokens // 16, 16, ffp), F32),
        g_rbox=V((zr, g, 8, 2 * ff), F32), g_lbox=V((zl, g, 8, 2 * ff), F32),
        h_rbox=V((zr, tg, 16, ffp), BF16), h_lbox=V((zl, tg, 16, ffp), BF16),
        h_stage=V((2, zr, tg, 16, ffp), BF16),
        hid=V((nz, tz, ffp), BF16), hg=V((nz, tz, ffp), BF16),
        ab=V((nz, 2 * tz, ffp), BF16), gr=V((2, nz, tz, ffp), BF16),
        st=V((2 * nz, 1, 128), F32),
        ly=V((ny, 8, 128), F32), lx=V((nx, 8, 128), F32),
        gd=V((ff, d_in), BF16), gw=V((2, ff, d_in), BF16),
    )
    gs = NSUB
    sm = dict(
        pair_sem=sems(1), tc_sem=sems(nx), sc_sem=sems(ny),
        txs_sem=sems(nx - 1), sxs_sem=sems(ny * (nx - 1)), tys_sem=sems(ny - 1), sys_sem=sems(ny - 1),
        ty_sem=sems(ny - 1), tx_sem=sems(ny * (nx - 1)), tk_sem=sems(nx),
        gy_sem=sems(ny - 1), gx_sem=sems(ny * (nx - 1)), gk_sem=sems(nx),
        gr_sem=sems(2 * zr * gs), gl_sem=sems(2 * zl * gs), hr_sem=sems(zr), hl_sem=sems(zl),
        pr_sem=sems(zr), pl_sem=sems(zl), wr_sem=sems(zr), wl_sem=sems(zl),
        ar_sem=sems(zr), al_sem=sems(zl),
        st_sem=sems(2 * nz - 1), ly_sem=sems(ny - 1), lx_sem=sems(nx - 1),
        load=DMA((6,)), out=DMA((3,)),
    )
    return {**vm, **sm}


def local(nz, ny, nx, student_in, teacher_hidden, proj, w_gate, w_up, w_down):
    w_gate, w_up = w_gate.T, w_up.T
    d_in = student_in.shape[1]
    ff = w_gate.shape[0]
    names = scratch(nz, ny, nx, d_in, proj.shape[0], ff)
    tree = jax.tree.structure(names)
    leaves = jax.tree.leaves(names)

    def kernel(*refs):
        s = jax.tree.unflatten(tree, refs[10:])
        body(nz, ny, nx, *refs[:10], s)

    any_spec = pl.BlockSpec(memory_space=pl.ANY)
    out = pl.pallas_call(
        kernel,
        out_shape=(
            jax.ShapeDtypeStruct((ff, d_in), BF16), jax.ShapeDtypeStruct((ff, d_in), BF16),
            jax.ShapeDtypeStruct((ff, d_in), BF16), jax.ShapeDtypeStruct((1, 1), F32)),
        in_specs=[any_spec] * 6,
        out_specs=(any_spec, any_spec, any_spec, pl.BlockSpec(memory_space=pltpu.VMEM)),
        scratch_shapes=leaves,
        compiler_params=pltpu.CompilerParams(
            collective_id=0, has_side_effects=True, vmem_limit_bytes=56 * 1024 * 1024),
        name="distill_step",
    )(student_in, teacher_hidden, proj, w_gate, w_up, w_down)
    return out[0].T, out[1].T, out[2], out[3].reshape(())


def solution(mesh):
    nz = mesh.shape["row"]
    chips = mesh.shape["col"] // 2
    nx = 4 if chips == 32 else 2
    ny = chips // nx
    return jax.shard_map(
        functools.partial(local, nz, ny, nx),
        mesh=mesh,
        in_specs=(
            P("col", "row"),
            P(None, "col"),
            P("col", "row"),
            P("row", "col"),
            P("row", "col"),
            P("col", "row"),
        ),
        out_specs=(P("row", "col"), P("row", "col"), P("col", "row"), P()),
        check_vma=False,
    )
```

```python
import functools

import jax
import jax.numpy as jnp
from jax import lax
from jax.experimental import pallas as pl
from jax.experimental.pallas import tpu as pltpu
from jax.sharding import PartitionSpec as P

BF16 = jnp.bfloat16
F32 = jnp.float32
MESH = pl.DeviceIdType.MESH
DMA = pltpu.SemaphoreType.DMA
NSUB = 4


def body(nz, ny, nx, si_h, th_h, proj_h, wg_h, wu_h, wd_h,
         gg_o, gu_o, gd_o, loss_o, s):
    zr = nz // 2
    zl = nz - 1 - zr
    tokens = ny * nx * 16
    grp = tokens // nz // 8
    tg = tokens // nz // 16
    tz = tokens // nz
    ff = wg_h.shape[0]
    ffp = s["wd"].shape[0]
    half = si_h.shape[1] // 2
    rows = 128 if tokens % 128 == 0 else tokens
    nrow = tokens // rows

    z = lax.axis_index("row")
    c = lax.axis_index("col")
    core = lax.rem(c, 2)
    other = 1 - core
    x = lax.rem(c // 2, nx)
    y = c // (2 * nx)

    def wrap(v, n):
        return lax.rem(v + 2 * n, n)

    def col(yy, xx, cc):
        return (yy * nx + xx) * 2 + cc

    partner = (z, col(y, x, other))
    right = (wrap(z + 1, nz), c)
    left = (wrap(z - 1, nz), c)

    def ypeer(d):
        return (z, col(wrap(y + d, ny), x, core))

    def xpeer(e):
        return (z, col(y, wrap(x + e, nx), core))

    def zpeer(d):
        return (wrap(z + d, nz), c)

    sent = []

    def send(src, dst, sems, at, device):
        send_sem, recv_sem = sems
        copy = pltpu.make_async_remote_copy(
            src_ref=src, dst_ref=dst, send_sem=send_sem.at[at], recv_sem=recv_sem.at[at],
            device_id=device, device_id_type=MESH)
        copy.start()
        sent.append(copy)
        return copy

    def flat(value):
        return value.reshape((-1, value.shape[-1]))

    loads = []
    for k, (src, dst) in enumerate((
            (si_h, s["si"]), (th_h, s["th"]), (proj_h, s["proj"]),
            (wg_h, s["wcat"].at[0:ff]), (wu_h, s["wcat"].at[ff:2 * ff]), (wd_h, s["wd"].at[0:ff]))):
        copy = pltpu.make_async_copy(src, dst, s["load"].at[k])
        copy.start()
        loads.append(copy)

    barrier = pltpu.get_barrier_semaphore()
    greet = [partner, right, left]
    greet += [ypeer(d) for d in range(1, ny)] + [xpeer(e) for e in range(1, nx)]
    greet += [zpeer(d) for d in sorted({2, nz - 2} - {1})]
    for device in greet:
        pl.semaphore_signal(barrier, inc=1, device_id=device, device_id_type=MESH)

    if ffp > ff:
        s["wd"][ff:ffp, :] = jnp.zeros((ffp - ff, 2 * half), BF16)
        s["hid"][z, :, ff:ffp] = jnp.zeros((s["hid"].shape[1], ffp - ff), BF16)
        s["ab"][z, :, ff:ffp] = jnp.zeros((s["ab"].shape[1], ffp - ff), BF16)

    loads[0].wait()
    own = s["si"][...].astype(F32)
    s["pair_out"][...] = jnp.where(core == 0, own[:, half:], own[:, :half])
    s["pair"][core] = jnp.where(core == 0, own[:, :half], own[:, half:])
    pl.semaphore_wait(barrier, len(greet))
    pair_copy = send(s["pair_out"], s["pair"].at[core], s["pair_sem"], 0, partner)

    loads[1].wait()
    loads[2].wait()

    def teach_half(h):
        weights = s["proj"][:, pl.ds(pl.multiple_of(h * half, 128), half)]

        def tile(m, carry):
            start = pl.multiple_of(m * rows, rows)
            part = jnp.dot(s["th"][pl.ds(start, rows), :], weights, preferred_element_type=F32)
            s["tp"][h, pl.ds(m * (ny // nrow), ny // nrow)] = part.reshape((ny // nrow, nx, 16, half))
            return carry

        lax.fori_loop(0, nrow, tile, 0)

    def pair_stage(part, inbox, sems):
        return [send(part.at[other, :, wrap(x + e, nx)], inbox.at[:, wrap(x + e, nx)], sems, e, partner)
                for e in range(nx)]

    def x_stage(part, inbox, outbox, box, sems, pair_copies):
        copies = []
        for e in list(range(1, nx)) + [0]:
            group = wrap(x + e, nx)
            pair_copies[e].wait_recv()
            total = part[core, :, group] + inbox[:, group]
            if e == 0:
                outbox[0] = total
            else:
                outbox[e] = total
                copies.append(send(outbox.at[e], box.at[e - 1], sems, e - 1, xpeer(e)))
        return copies

    def y_stage(outbox, box, sums, ybox, sems, copies):
        for copy in copies:
            copy.wait_recv()
        total = outbox[0]
        for e in range(1, nx):
            total = total + box[e - 1]
        sums[...] = total
        return [send(sums.at[wrap(y + d, ny)], ybox.at[d - 1], sems, d - 1, ypeer(d)) for d in range(1, ny)]

    def y_total(sums, ybox, copies):
        for copy in copies:
            copy.wait_recv()
        total = sums[y]
        for d in range(1, ny):
            total = total + ybox[d - 1]
        return total

    teach_half(other)
    teach_pair = pair_stage(s["tp"], s["t_in"], s["tc_sem"])
    teach_half(core)

    def gather_start(buf, sems):
        y_sems, x_sems, _ = sems
        y_copies = [send(buf.at[core, y, x], buf.at[core, y, x], y_sems, d - 1, ypeer(d)) for d in range(1, ny)]
        x_copies = [[send(buf.at[core, y, x], buf.at[core, y, x], x_sems, e - 1, xpeer(e)) for e in range(1, nx)]]
        return y_copies, x_copies

    def gather_finish(buf, sems, started):
        y_copies, x_copies = started
        _, x_sems, c_sems = sems
        order = sorted(range(1, ny), key=lambda d: min(d, ny - d))
        for d in order:
            y_copies[d - 1].wait_recv()
            block = buf.at[core, wrap(y - d, ny), x]
            x_copies.append([send(block, block, x_sems, d * (nx - 1) + e - 1, xpeer(e)) for e in range(1, nx)])
        c_copies = [send(buf.at[core, :, x], buf.at[core, :, x], c_sems, 0, partner)]
        for e in sorted(range(1, nx), key=lambda e: min(e, nx - e)):
            for copies in x_copies:
                copies[e - 1].wait_recv()
            block = buf.at[core, :, wrap(x - e, nx)]
            c_copies.append(send(block, block, c_sems, e, partner))
        for copy in c_copies:
            copy.wait_recv()

    pair_copy.wait_recv()
    s["tok"][core, y, x] = flat(s["pair"][...]).astype(BF16)
    tok_sems = (s["ty_sem"], s["tx_sem"], s["tk_sem"])
    started = gather_start(s["tok"], tok_sems)
    gather_finish(s["tok"], tok_sems, started)

    loads[3].wait()
    loads[4].wait()
    yrow = ny // nrow
    nt = (((1,), (1,)), ((), ()))

    def gate_tile(m, carry):
        at = pl.ds(m * yrow, yrow)
        part = lax.dot_general(flat(s["tok"][0, at]), s["wcat"][:, 0:half], nt, preferred_element_type=F32)
        part += lax.dot_general(flat(s["tok"][1, at]), s["wcat"][:, half:2 * half], nt, preferred_element_type=F32)
        s["gp"][pl.ds(m * (rows // 8), rows // 8)] = part.reshape((rows // 8, 8, 2 * ff))
        return carry

    lax.fori_loop(0, nrow, gate_tile, 0)

    def ring_reduce(part, rbox, lbox, sems, nsub, between):
        r_sems, l_sems = sems
        size = grp // nsub

        def chunk(j, q):
            return pl.ds(wrap(j, nz) * grp + q * size, size)

        def piece(step, q):
            return (step, pl.ds(q * size, size))

        r_copies, l_copies = [], []
        for q in range(nsub):
            r_copies.append(send(part.at[chunk(z + zr, q)], rbox.at[piece(0, q)], r_sems, q, right))
            l_copies.append(send(part.at[chunk(z - zl, q)], lbox.at[piece(0, q)], l_sems, q, left))
        for step in range(1, zr):
            between(step)
            for q in range(nsub):
                was, now = piece(step - 1, q), piece(step, q)
                at = step * nsub + q
                r_copies[q].wait_recv()
                rbox[was] = rbox[was] + part[chunk(z + zr - step, q)]
                r_copies[q] = send(rbox.at[was], rbox.at[now], r_sems, at, right)
                if step < zl:
                    l_copies[q].wait_recv()
                    lbox[was] = lbox[was] + part[chunk(z - zl + step, q)]
                    l_copies[q] = send(lbox.at[was], lbox.at[now], l_sems, at, left)
        for q in range(nsub):
            l_copies[q].wait_recv()
            r_copies[q].wait_recv()
        total = part[pl.ds(z * grp, grp)] + rbox[zr - 1] + lbox[zl - 1]
        return flat(total)

    def skip_gather(buf, sems):
        copies = [{}, {}]
        sides = ((0, 1, zr), (1, -1, zl))

        def spread(side, sign, reach, distance):
            block = buf.at[wrap(z - sign * distance, nz)]
            for hop in (2, 1):
                if distance + hop <= reach:
                    copies[side][distance + hop] = send(
                        block, block, sems[side], distance + hop - 1, zpeer(sign * hop))

        for side in sides:
            spread(*side, 0)
        yield
        for distance in range(2, zr + 1, 2):
            for side, sign, reach in sides:
                if distance <= reach:
                    copies[side][distance].wait_recv()
                    spread(side, sign, reach, distance)
            yield
        for side, sign, reach in sides:
            for distance in range(1, reach + 1, 2):
                copies[side][distance].wait_recv()

    def skip_reduce(part, stage, boxes, sems, between):
        copies = [{}, {}]
        sides = ((0, 1, zr), (1, -1, zl))

        def own(j):
            return part[pl.ds(wrap(j, nz) * tg, tg)]

        def arrived(side, reach, distance):
            total = 0.0
            for hop in (1, 2):
                if distance + hop <= reach:
                    copies[side][distance + hop].wait_recv()
                    total = total + boxes[side][distance + hop - 1].astype(F32)
            return total

        def launch(side, sign, distance, value):
            hop = 2 - distance % 2
            stage[side, distance - 1] = value.astype(BF16)
            copies[side][distance] = send(
                stage.at[side, distance - 1], boxes[side].at[distance - 1], sems[side], distance - 1, zpeer(sign * hop))

        for side, sign, reach in sides:
            if reach % 2 == 0:
                launch(side, sign, reach, own(z + sign * reach))
        for distance in range(zr - 1 + zr % 2, 0, -2):
            for side, sign, reach in sides:
                if distance <= reach:
                    launch(side, sign, distance, own(z + sign * distance))
        step = 0
        for distance in range(zr, 1, -2):
            step += 1
            for side, sign, reach in sides:
                if distance < reach:
                    launch(side, sign, distance, own(z + sign * distance) + arrived(side, reach, distance))
            between(step)
        total = own(z)
        for side, sign, reach in sides:
            total = total + arrived(side, reach, 0)
        return flat(total)

    teach_x, y_copies = [], []

    def teach_between(step):
        if step == 1:
            teach_x.extend(x_stage(s["tp"], s["t_in"], s["t_out"], s["t_box"], s["txs_sem"], teach_pair))
        if step == zr - 1:
            y_copies.extend(y_stage(s["t_out"], s["t_box"], s["t_sum"], s["t_ybox"], s["tys_sem"], teach_x))

    gate_up = ring_reduce(s["gp"], s["g_rbox"], s["g_lbox"], (s["gr_sem"], s["gl_sem"]), NSUB, teach_between)
    gate_val = gate_up[:, 0:ff]
    up_val = gate_up[:, ff:2 * ff]
    logistic = 1.0 / (1.0 + jnp.exp(-gate_val))
    silu_gate = gate_val * logistic
    s["hid"][z, :, 0:ff] = (silu_gate * up_val).astype(BF16)
    gather = skip_gather(s["hid"], (s["hr_sem"], s["hl_sem"]))
    next(gather)
    slope = up_val * (logistic * (1.0 + gate_val * (1.0 - logistic)))
    s["ab"][z, 0:tz, 0:ff] = slope.astype(BF16)
    s["ab"][z, tz:2 * tz, 0:ff] = silu_gate.astype(BF16)
    loads[5].wait()
    next(gather)
    s["teach"][...] = y_total(s["t_sum"], s["t_ybox"], y_copies)
    for _ in gather:
        pass

    zrow = nz // nrow

    def stud_half(h):
        weights = s["wd"][:, pl.ds(pl.multiple_of(h * half, 128), half)]

        def tile(m, carry):
            part = jnp.dot(flat(s["hid"][pl.ds(m * zrow, zrow)]), weights, preferred_element_type=F32)
            s["sp"][h, pl.ds(m * yrow, yrow)] = part.reshape((yrow, nx, 16, half))
            return carry

        lax.fori_loop(0, nrow, tile, 0)

    factors = skip_gather(s["ab"], (s["ar_sem"], s["al_sem"]))
    order = sorted(range(ny), key=lambda d: -min(d, ny - d))
    stud_half(other)
    pair_copies = {}
    for d in order:
        yy = wrap(y + d, ny)
        pair_copies[d] = send(s["sp"].at[other, yy], s["s_in"].at[yy], s["sc_sem"], d, partner)
    next(factors)
    stud_half(core)
    x_copies = {}

    def x_send(d, e, value, slot, device):
        yy = wrap(y + d, ny)
        s["s_out"][e, yy] = value
        x_copies[d, slot] = send(s["s_out"].at[e, yy], s["s_box"].at[slot, yy], s["sxs_sem"], d * 3 + slot, device)

    def x_own(d, e):
        yy = wrap(y + d, ny)
        xx = wrap(x + e, nx)
        return s["sp"][core, yy, xx] + s["s_in"][yy, xx]

    for d in order:
        pair_copies[d].wait_recv()
        if nx == 4:
            x_send(d, 2, x_own(d, 2), 2, xpeer(1 if d % 2 == 0 else 3))
            slot, e = (1, 3) if d % 2 == 0 else (0, 1)
            x_send(d, e, x_own(d, e), slot, xpeer(e))
        else:
            x_send(d, 1, x_own(d, 1), 0, xpeer(1))
        s["s_out"][0, wrap(y + d, ny)] = x_own(d, 0)
    if nx == 4:
        for d in order:
            slot, e = (0, 1) if d % 2 == 0 else (1, 3)
            x_copies[d, 2].wait_recv()
            x_send(d, e, x_own(d, e) + s["s_box"][2, wrap(y + d, ny)], slot, xpeer(e))
    next(factors)
    stud_y = []
    for d in order:
        yy = wrap(y + d, ny)
        total = s["s_out"][0, yy]
        for slot in range(2 if nx == 4 else 1):
            x_copies[d, slot].wait_recv()
            total = total + s["s_box"][slot, yy]
        s["s_sum"][yy] = total
        if d:
            stud_y.append((d, send(s["s_sum"].at[yy], s["s_ybox"].at[d - 1], s["sys_sem"], d - 1, ypeer(d))))
    stud_y = [copy for _, copy in sorted(stud_y, key=lambda pair: pair[0])]
    if zr > 2:
        next(factors)

    teacher = s["teach"][...]
    teach_max = jnp.max(teacher, axis=1, keepdims=True)
    teach_exp = jnp.exp(teacher - teach_max)
    teach_norm = jnp.sum(teach_exp, axis=1, keepdims=True)

    student = flat(s["pair"][...]) + y_total(s["s_sum"], s["s_ybox"], stud_y)
    stud_max = jnp.max(student, axis=1, keepdims=True)
    stud_norm = jnp.sum(jnp.exp(student - stud_max), axis=1, keepdims=True)
    cross = jnp.sum(teach_exp * student, axis=1, keepdims=True)

    lane = lax.broadcasted_iota(jnp.int32, (16, 128), 1)
    stats = jnp.where(lane == 0, stud_max, jnp.where(lane == 1, teach_max, jnp.where(
        lane == 2, stud_norm, jnp.where(lane == 3, teach_norm, cross))))
    stats = jnp.concatenate([stats, jnp.zeros((112, 128), F32)], axis=0).T[0:8]
    line = stats[0:1]
    for k in range(1, 5):
        line = line + pltpu.roll(stats, 16 * k, 1)[k:k + 1]
    mine = 2 * z + core
    s["st"][mine] = line
    st_copies = []
    for d in range(nz):
        for k, cc in enumerate((core, other)):
            if d or k:
                st_copies.append(send(s["st"].at[mine], s["st"].at[mine], s["st_sem"], 2 * d + k - 1,
                                      (wrap(z + d, nz), col(y, x, cc))))
    if zr > 3:
        next(factors)
    for copy in st_copies:
        copy.wait_recv()
    lines = s["st"][...].reshape((2 * nz, 128))
    top = jnp.max(lines, axis=0, keepdims=True)
    scale = jnp.exp(lines - top)
    wide = lax.broadcasted_iota(jnp.int32, (2 * nz, 128), 1)
    scale = jnp.where(wide < 64, pltpu.roll(scale, 32, 1), pltpu.roll(scale, 48, 1))
    total = jnp.sum(lines * scale, axis=0, keepdims=True)
    row = lax.broadcasted_iota(jnp.int32, (8, 128), 0)
    line = jnp.broadcast_to(jnp.where(wide[0:1] < 32, top, total), (8, 128))
    stats = line
    for k in range(1, 5):
        stats = jnp.where(row == k, pltpu.roll(line, 128 - 16 * k, 1), stats)
    stats = jnp.concatenate([stats, jnp.zeros((120, 128), F32)], axis=0).T[0:16]
    stud_max = stats[:, 0:1]
    teach_max = stats[:, 1:2]
    stud_norm = stats[:, 2:3]
    teach_norm = stats[:, 3:4]
    cross = stats[:, 4:5]

    stud_grad = jnp.exp(student - stud_max) / stud_norm - jnp.exp(teacher - teach_max) / teach_norm
    s["sg"][core, y, x] = stud_grad.astype(BF16)
    sg_sems = (s["gy_sem"], s["gx_sem"], s["gk_sem"])
    started = gather_start(s["sg"], sg_sems)
    token_loss = stud_max + jnp.log(stud_norm) - cross / teach_norm
    own_loss = jnp.sum(token_loss, axis=0, keepdims=True) * (1.0 / tokens)
    s["ly"][y] = jnp.broadcast_to(own_loss, (8, 128))
    ly_copies = [send(s["ly"].at[y], s["ly"].at[y], s["ly_sem"], d - 1, ypeer(d)) for d in range(1, ny)]
    gather_finish(s["sg"], sg_sems, started)

    def grad_tile(m, carry):
        at = pl.ds(m * yrow, yrow)
        part = lax.dot_general(flat(s["sg"][0, at]), s["wd"][:, 0:half], nt, preferred_element_type=F32)
        part += lax.dot_general(flat(s["sg"][1, at]), s["wd"][:, half:2 * half], nt, preferred_element_type=F32)
        s["hp"][pl.ds(m * (rows // 16), rows // 16)] = part.reshape((rows // 16, 16, ffp))
        return carry

    lax.fori_loop(0, nrow, grad_tile, 0)

    tn = (((0,), (0,)), ((), ()))
    lx_copies = []

    def down_between(step):
        if step <= 2:
            h = step - 1
            s["gd"][:, h * half:(h + 1) * half] = lax.dot_general(
                flat(s["hid"][...]), flat(s["sg"][h]), tn, preferred_element_type=F32).astype(BF16)[0:ff]
        if step == zr // 2:
            for copy in ly_copies:
                copy.wait_recv()
            s["lx"][x] = functools.reduce(lambda a, b: a + b, [s["ly"][k] for k in range(ny)])
            lx_copies.extend(send(s["lx"].at[x], s["lx"].at[x], s["lx_sem"], e - 1, xpeer(e)) for e in range(1, nx))

    hidden_grad = skip_reduce(s["hp"], s["h_stage"], (s["h_rbox"], s["h_lbox"]),
                              (s["pr_sem"], s["pl_sem"]), down_between)
    s["hg"][z] = hidden_grad.astype(BF16)
    gather = skip_gather(s["hg"], (s["wr_sem"], s["wl_sem"]))
    next(gather)
    for _ in factors:
        pass
    if zr < 4:
        for h in range(zr // 2, 2):
            down_between(h + 1)
    out = pltpu.make_async_copy(s["gd"], gd_o, s["out"].at[0])
    out.start()
    loads.append(out)
    next(gather)
    for copy in lx_copies:
        copy.wait_recv()
    loss = functools.reduce(lambda a, b: a + b, [s["lx"][k] for k in range(nx)])
    loss_o[...] = loss[0:1, 0:1]
    for _ in gather:
        pass

    def factor_tile(m, carry):
        at = pl.ds(m * zrow, zrow)
        grad = s["hg"][at].astype(F32)
        for k in range(2):
            factor = s["ab"][at, k * tz:(k + 1) * tz].astype(F32)
            s["gr"][k, at] = (grad * factor).astype(BF16)
        return carry

    lax.fori_loop(0, nrow, factor_tile, 0)

    outs = []
    for k, dst in enumerate((gg_o, gu_o)):
        for h in range(2):
            s["gw"][k, :, h * half:(h + 1) * half] = lax.dot_general(
                flat(s["gr"][k]), flat(s["tok"][h]), tn, preferred_element_type=F32).astype(BF16)[0:ff]
        out = pltpu.make_async_copy(s["gw"].at[k], dst, s["out"].at[1 + k])
        out.start()
        outs.append(out)
    for copy in sent:
        copy.wait_send()
    loads[6].wait()
    for out in outs:
        out.wait()


def scratch(nz, ny, nx, d_in, k_in, ff):
    zr = nz // 2
    zl = nz - 1 - zr
    tokens = ny * nx * 16
    half = d_in // 2
    tz = tokens // nz
    g = tz // 8
    tg = tz // 16
    ffp = -(-ff // 128) * 128
    V = pltpu.VMEM

    def sems(*n):
        return (DMA(n), DMA(n))

    vm = dict(
        si=V((8, d_in), BF16), th=V((tokens, k_in), BF16), proj=V((k_in, d_in), BF16),
        wcat=V((2 * ff, d_in), BF16), wd=V((ffp, d_in), BF16),
        pair_out=V((8, half), F32), pair=V((2, 8, half), F32),
        tok=V((2, ny, nx, 16, half), BF16), sg=V((2, ny, nx, 16, half), BF16),
        tp=V((2, ny, nx, 16, half), F32), sp=V((2, ny, nx, 16, half), F32),
        t_in=V((ny, nx, 16, half), F32), s_in=V((ny, nx, 16, half), F32),
        t_out=V((nx, ny, 16, half), F32), s_out=V((nx, ny, 16, half), F32),
        t_box=V((nx - 1, ny, 16, half), F32), s_box=V((nx - 1, ny, 16, half), F32),
        t_sum=V((ny, 16, half), F32), s_sum=V((ny, 16, half), F32),
        t_ybox=V((ny - 1, 16, half), F32), s_ybox=V((ny - 1, 16, half), F32),
        teach=V((16, half), F32),
        gp=V((tokens // 8, 8, 2 * ff), F32), hp=V((tokens // 16, 16, ffp), F32),
        g_rbox=V((zr, g, 8, 2 * ff), F32), g_lbox=V((zl, g, 8, 2 * ff), F32),
        h_rbox=V((zr, tg, 16, ffp), BF16), h_lbox=V((zl, tg, 16, ffp), BF16),
        h_stage=V((2, zr, tg, 16, ffp), BF16),
        hid=V((nz, tz, ffp), BF16), hg=V((nz, tz, ffp), BF16),
        ab=V((nz, 2 * tz, ffp), BF16), gr=V((2, nz, tz, ffp), BF16),
        st=V((2 * nz, 1, 128), F32),
        ly=V((ny, 8, 128), F32), lx=V((nx, 8, 128), F32),
        gd=V((ff, d_in), BF16), gw=V((2, ff, d_in), BF16),
    )
    gs = NSUB
    sm = dict(
        pair_sem=sems(1), tc_sem=sems(nx), sc_sem=sems(ny),
        txs_sem=sems(nx - 1), sxs_sem=sems(ny * 3), tys_sem=sems(ny - 1), sys_sem=sems(ny - 1),
        ty_sem=sems(ny - 1), tx_sem=sems(ny * (nx - 1)), tk_sem=sems(nx),
        gy_sem=sems(ny - 1), gx_sem=sems(ny * (nx - 1)), gk_sem=sems(nx),
        gr_sem=sems(zr * gs), gl_sem=sems(zl * gs), hr_sem=sems(zr), hl_sem=sems(zl),
        pr_sem=sems(zr), pl_sem=sems(zl), wr_sem=sems(zr), wl_sem=sems(zl),
        ar_sem=sems(zr), al_sem=sems(zl),
        st_sem=sems(2 * nz - 1), ly_sem=sems(ny - 1), lx_sem=sems(nx - 1),
        load=DMA((6,)), out=DMA((3,)),
    )
    return {**vm, **sm}


def local(nz, ny, nx, student_in, teacher_hidden, proj, w_gate, w_up, w_down):
    w_gate, w_up = w_gate.T, w_up.T
    d_in = student_in.shape[1]
    ff = w_gate.shape[0]
    names = scratch(nz, ny, nx, d_in, proj.shape[0], ff)
    tree = jax.tree.structure(names)
    leaves = jax.tree.leaves(names)

    def kernel(*refs):
        s = jax.tree.unflatten(tree, refs[10:])
        body(nz, ny, nx, *refs[:10], s)

    any_spec = pl.BlockSpec(memory_space=pl.ANY)
    out = pl.pallas_call(
        kernel,
        out_shape=(
            jax.ShapeDtypeStruct((ff, d_in), BF16), jax.ShapeDtypeStruct((ff, d_in), BF16),
            jax.ShapeDtypeStruct((ff, d_in), BF16), jax.ShapeDtypeStruct((1, 1), F32)),
        in_specs=[any_spec] * 6,
        out_specs=(any_spec, any_spec, any_spec, pl.BlockSpec(memory_space=pltpu.VMEM)),
        scratch_shapes=leaves,
        compiler_params=pltpu.CompilerParams(
            collective_id=0, has_side_effects=True, vmem_limit_bytes=56 * 1024 * 1024),
        name="distill_step",
    )(student_in, teacher_hidden, proj, w_gate, w_up, w_down)
    return out[0].T, out[1].T, out[2], out[3].reshape(())


def solution(mesh):
    nz = mesh.shape["row"]
    chips = mesh.shape["col"] // 2
    nx = 4 if chips % 8 == 0 else 2
    ny = chips // nx
    return jax.shard_map(
        functools.partial(local, nz, ny, nx),
        mesh=mesh,
        in_specs=(
            P("col", "row"),
            P(None, "col"),
            P("col", "row"),
            P("row", "col"),
            P("row", "col"),
            P("col", "row"),
        ),
        out_specs=(P("row", "col"), P("row", "col"), P("col", "row"), P()),
        check_vma=False,
    )
```
